32 devices in a mesh: depth: 16 (over z, y, x), batch: 2 (over core).
Axes of the slice: x: 2, y: 2, z: 4, core: 2. Of those that a mesh axis runs over, the one named last changes fastest.
Arguments:
- inputs: float32 [4, 64, 512], P('batch'), parts along dimension 0, may hold values from -6 to 6
- attn_in: bfloat16 [16, 512, 1536], P('depth'), may hold values from -0.25 to 0.25
- attn_out: bfloat16 [16, 512, 512], P('depth'), may hold values from -0.25 to 0.25
- mlp_in: bfloat16 [16, 512, 1024], P('depth'), may hold values from -0.25 to 0.25
- mlp_out: bfloat16 [16, 1024, 512], P('depth'), may hold values from -0.1875 to 0.1875
- norm_gain: float32 [16, 512], P('depth'), may hold values from 0.25 to 1.75
- head_gain: float32 [16, 64], P('depth'), may hold values from 0.25 to 1.75
Outputs:
- states: float32 [16, 4, 64, 512], P('depth', 'batch'), parts along dimension 1
- coarse_points: float32 [16, 4, 64, 512], P('depth', 'batch'), parts along dimension 1
The draws below stay inside these ranges and needn't reach their ends.
There are 2 independent parts, one for each index of `batch`. The reference program is written for one: setup_inputs(seed, part) draws one part's arguments, and reference() takes and returns one part's arrays. A program takes and returns all parts, laid end to end along the dimension named above; an argument that names none is the same for every part. Nothing has to cross between parts.
All inputs are finite; a program needn't handle non-finite values.
Results may differ from the reference program's by a relative error of at most 0.014.
Values sent between devices are 32-bit elements; how exact they have to be, the bound alone decides.
A program may use at most 64 MiB of HBM per device.

```python
import math
import jax
import jax.numpy as jnp
from jax import lax

D = 512
HEAD_DIM = 64
FF = 1024
FRAMES = 64
MICRO = 2
COARSEN = 4
LAYERS = 16


def steps_of(own_key, extent, pieces, least, high):
    def one(position, parts):
        heights = jax.random.uniform(jax.random.fold_in(jax.random.fold_in(own_key, 6), position), (parts,), jnp.float32, least / len(pieces), high / len(pieces))
        return jnp.repeat(jnp.exp(heights), extent[position] // parts).reshape((-1,) + (1,) * (len(extent) - position - 1))

    gain = one(*pieces[0])
    for cut in pieces[1:]:
        gain = gain * one(*cut)
    return gain


def noise(stream_key, extent, width, bound, split=(), kind=jnp.bfloat16):
    array = width * jax.random.normal(stream_key, extent, jnp.float32)
    if split:
        array = array * steps_of(stream_key, extent, split, -0.22, 0.18)
    return jnp.clip(array, -bound, bound).astype(kind)


def setup_inputs(seed: int = 0, part: int = 0) -> dict:
    streams_of = jax.random.split(jax.random.key(seed), 8)
    part_splits = jax.random.split(jax.random.fold_in(streams_of[7], part), 8)
    inputs = noise(part_splits[0], (MICRO, FRAMES, D), 1.0, 6.0, (), jnp.float32)
    attn_in = noise(streams_of[1], (LAYERS, D, 3 * D), D ** -0.5, 0.25, ((0, 16),))
    attn_out = noise(streams_of[2], (LAYERS, D, D), D ** -0.5, 0.25, ((0, 16),))
    mlp_in = noise(streams_of[3], (LAYERS, D, FF), D ** -0.5, 0.25, ((0, 16),))
    mlp_out = noise(streams_of[4], (LAYERS, FF, D), FF ** -0.5, 0.1875, ((0, 16),))
    norm_gain = jnp.clip(1.0 + 0.15 * jax.random.normal(streams_of[5], (LAYERS, D), jnp.float32), 0.25, 1.75)
    head_gain = jnp.clip(1.0 + 0.15 * jax.random.normal(streams_of[6], (LAYERS, HEAD_DIM), jnp.float32), 0.25, 1.75)
    return {"inputs": inputs, "attn_in": attn_in, "attn_out": attn_out, "mlp_in": mlp_in, "mlp_out": mlp_out, "norm_gain": norm_gain, "head_gain": head_gain}


step_size = 0.25
epsilon = 1e-06

def normalize(values):
    return values * lax.rsqrt(lax.optimization_barrier(jnp.mean(values * values, axis=-1, keepdims=True)) + epsilon)

def layer_delta(current, w_qkv, w_out, w_up, w_down, in_gain, qk_gain):
    batch_size, frame_count, model_width = current.shape
    head_dim = qk_gain.shape[0]
    head_count = model_width // head_dim
    normed = (normalize(current) * in_gain).astype(jnp.bfloat16)
    projected = jnp.dot(normed, w_qkv, preferred_element_type=jnp.float32)
    projected = projected.reshape(batch_size, frame_count, 3, head_count, head_dim)
    query_rows = (normalize(projected[:, :, 0]) * qk_gain).astype(jnp.bfloat16)
    key_rows = (normalize(projected[:, :, 1]) * qk_gain).astype(jnp.bfloat16)
    value_rows = projected[:, :, 2].astype(jnp.bfloat16)
    scores = jnp.einsum('bqhe,bkhe->bhqk', query_rows.astype(jnp.float32), key_rows.astype(jnp.float32)) / math.sqrt(head_dim)
    causal = jnp.arange(frame_count)[:, None] >= jnp.arange(frame_count)[None, :]
    exp_scores = jnp.where(causal, jnp.exp(scores), 0.0)
    probs = (exp_scores / lax.optimization_barrier(jnp.sum(exp_scores, axis=-1, keepdims=True))).astype(jnp.bfloat16)
    context = jnp.einsum('bhqk,bkhe->bqhe', probs.astype(jnp.float32), value_rows.astype(jnp.float32))
    context = context.astype(jnp.bfloat16).reshape(batch_size, frame_count, model_width)
    attention = jnp.dot(context, w_out, preferred_element_type=jnp.float32)
    hidden = jax.nn.gelu(jnp.dot(normed, w_up, preferred_element_type=jnp.float32), approximate=True).astype(jnp.bfloat16)
    return attention + jnp.dot(hidden, w_down, preferred_element_type=jnp.float32)

def reference(inputs, attn_in, attn_out, mlp_in, mlp_out, norm_gain, head_gain):
    blocks = LAYERS // COARSEN
    stacked = (attn_in, attn_out, mlp_in, mlp_out, norm_gain, head_gain)
    grouped = tuple((item.reshape((blocks, COARSEN) + item.shape[1:]) for item in stacked))

    def slot_weights(slot):
        return tuple((item[:, slot] for item in grouped))
    apply_all = jax.vmap(layer_delta)
    apply_shared = jax.vmap(layer_delta, in_axes=(None, 0, 0, 0, 0, 0, 0))
    repeated = jnp.broadcast_to(inputs, (blocks,) + inputs.shape)
    moving = repeated
    base_sum = jnp.zeros_like(repeated)
    for slot in range(COARSEN):
        if slot == 0:
            change = apply_all(repeated, *slot_weights(0))
            base_sum = base_sum + change
        else:
            base_sum = base_sum + apply_all(repeated, *slot_weights(slot))
            change = apply_all(moving, *slot_weights(slot))
        moving = moving + step_size * change
    offsets = moving - repeated - step_size * base_sum

    def coarse_turn(current, item):
        offset, weights = item
        increments = apply_shared(current, *weights)
        following = offset + current + step_size * lax.optimization_barrier(jnp.sum(increments, axis=0))
        return (following, following)
    later = lax.scan(coarse_turn, inputs, (offsets, grouped))[1]
    starts = jnp.concatenate([inputs[None], later[:-1]], axis=0)
    moving = starts
    for slot in range(COARSEN):
        moving = moving + step_size * apply_all(moving, *slot_weights(slot))
    fresh = moving
    moving = jnp.concatenate([inputs[None], fresh[:-1]], axis=0)
    finals = []
    for slot in range(COARSEN - 1):
        moving = moving + step_size * apply_all(moving, *slot_weights(slot))
        finals.append(moving)
    result = jnp.stack(finals + [fresh], axis=1).reshape((LAYERS,) + inputs.shape)
    coarse_points = jnp.repeat(later, COARSEN, axis=0)
    return (result, coarse_points)
```

```python
import functools
import math

import jax
import jax.numpy as jnp
from jax import lax
from jax.experimental import pallas as pl
from jax.experimental.pallas import tpu as pltpu
from jax.sharding import PartitionSpec as P

COARSEN = 4
GROUP = 256
PIECES = 2
LAG = 2

step_size = 0.25
epsilon = 1e-06

FIRST, CHAIN, COARSE, RELAX, FINAL = range(5)
STAGES = 5
MESH = pl.DeviceIdType.MESH


def kernel(
    blocks, inputs, h_qkv, h_out, h_up, h_down, h_gain, h_head, states, coarse,
    w_qkv, w_out, w_up, w_down, in_gain, qk_gain, keys_ref, values_ref, load_sem, rx, tx, base, ends, term, share, parts, gathered, same_head, head_scale, query_scale,
    send_sem, recv_sem, share_send, share_recv, ahead_send, own_send, own_recv, back_send,
):
    micro, frames, width = inputs.shape
    head_dim = qk_gain.shape[1]
    rows = frames // COARSEN
    device = lax.axis_index("depth")
    position = lax.rem(device, COARSEN)
    block = device // COARSEN
    has_next = block < blocks - 1
    last = COARSEN - 1
    is_last = position == last

    loads = [
        pltpu.make_async_copy(source, target, load_sem.at[i])
        for i, (source, target) in enumerate((
            (h_head, qk_gain), (h_gain, in_gain), (inputs, rx.at[FIRST]), (h_qkv, w_qkv),
            (h_up, w_up), (h_out, w_out), (h_down, w_down),
        ))
    ]
    for load in loads:
        load.start()

    def at(depth):
        return {"depth": depth}

    barrier = pltpu.get_barrier_semaphore()
    for i in range(COARSEN):
        @pl.when(block > 0)
        def _():
            pl.semaphore_signal(barrier, inc=1, device_id=at((block - 1) * COARSEN + i), device_id_type=MESH)

        @pl.when(has_next)
        def _():
            pl.semaphore_signal(barrier, inc=1, device_id=at((block + 1) * COARSEN + i), device_id_type=MESH)

    for i in range(1, COARSEN):
        other = block * COARSEN + lax.rem(position + i, COARSEN)
        pl.semaphore_signal(barrier, inc=1, device_id=at(other), device_id_type=MESH)

    heads_of = lax.broadcasted_iota(jnp.int32, (GROUP, GROUP), 0) // head_dim
    heads_at = lax.broadcasted_iota(jnp.int32, (GROUP, GROUP), 1) // head_dim
    same_head[...] = jnp.where(heads_of == heads_at, 1.0, 0.0).astype(jnp.bfloat16)
    keys_ref[...] = jnp.zeros_like(keys_ref)
    values_ref[...] = jnp.zeros_like(values_ref)
    loads[0].wait()
    head_scale[...] = jnp.concatenate([qk_gain[...]] * (width // head_dim), axis=1)
    query_scale[...] = head_scale[...] * (1.0 / math.sqrt(head_dim))

    neighbours = (block > 0).astype(jnp.int32) + has_next.astype(jnp.int32)
    pl.semaphore_wait(barrier, COARSEN - 1 + COARSEN * neighbours)

    for load in loads[1:]:
        load.wait()

    def delta(current, unit):
        piece = lax.rem(unit, PIECES)
        here = pl.ds(pl.multiple_of(piece * frames, frames), frames)
        spread = jnp.mean(current * current, axis=-1, keepdims=True) + epsilon
        row_scale = lax.rsqrt(spread)
        gained = (current * in_gain[...]).astype(jnp.bfloat16)
        same = same_head[...]
        copies = GROUP // head_dim
        causal = lax.broadcasted_iota(jnp.int32, (frames, GROUP), 0) + piece * frames >= lax.rem(
            lax.broadcasted_iota(jnp.int32, (frames, GROUP), 1), PIECES * frames
        )
        starts = range(0, width, GROUP)
        half = w_up.shape[2] // 2

        def project(part):
            return jnp.dot(
                gained, w_qkv[0, :, part * width:(part + 1) * width], preferred_element_type=jnp.float32
            )

        def head_norm(rows_of, scale_of):
            cut = [rows_of[:, start:start + GROUP] for start in starts]
            squares = jnp.concatenate([(part * part).astype(jnp.bfloat16) for part in cut], axis=0)
            means = jnp.dot(squares, same, preferred_element_type=jnp.float32) * (1.0 / head_dim)
            scales = lax.rsqrt(means + jnp.concatenate([epsilon * spread] * len(cut), axis=0))
            return [
                (part * (scales[i * frames:(i + 1) * frames] * scale_of[:, start:start + GROUP])).astype(jnp.bfloat16)
                for i, (part, start) in enumerate(zip(cut, starts))
            ]

        def raise_half(i):
            raised = jnp.dot(gained, w_up[0, :, i * half:(i + 1) * half], preferred_element_type=jnp.float32)
            return jax.nn.gelu(raised * row_scale, approximate=True).astype(jnp.bfloat16)

        def lower_half(i, hidden):
            return jnp.dot(hidden, w_down[0, i * half:(i + 1) * half], preferred_element_type=jnp.float32)

        key_rows = project(1)
        query_rows = project(0)
        keys_of = head_norm(key_rows, head_scale)
        queries_of = head_norm(query_rows, query_scale)
        values_of = (project(2) * row_scale).astype(jnp.bfloat16)
        hidden = raise_half(0)
        weights, mixes = [], []
        for i, start in enumerate(starts):
            part = slice(start, start + GROUP)
            keys_ref[here, part] = keys_of[i]
            values_ref[here, part] = values_of[:, part]
            keys = jnp.concatenate([keys_ref[:, part]] * copies, axis=0) * same
            scores = lax.dot_general(
                queries_of[i], keys, (((1,), (1,)), ((), ())), preferred_element_type=jnp.float32
            )
            weights.append(jnp.where(causal, jnp.exp(scores), 0.0).astype(jnp.bfloat16))
        late = raise_half(1)
        lowered = lower_half(0, hidden)
        for weight, start in zip(weights, starts):
            values = jnp.concatenate([values_ref[:, start:start + GROUP]] * copies, axis=0) * same
            mixes.append(jnp.dot(weight, values, preferred_element_type=jnp.float32))
        totals = jnp.dot(jnp.concatenate(weights, axis=0), same, preferred_element_type=jnp.float32)
        lowered = lowered + lower_half(1, late)
        contexts = [
            (mixed / totals[i * frames:(i + 1) * frames]).astype(jnp.bfloat16)
            for i, mixed in enumerate(mixes)
        ]
        context = jnp.concatenate(contexts, axis=1)
        return jnp.dot(context, w_out[0], preferred_element_type=jnp.float32) + lowered

    def active(stage):
        return (
            ((stage == FIRST) & ((block > 0) | (position == 0)))
            | ((stage == CHAIN) & (position > 0))
            | ((stage == COARSE) & (block > 0))
            | ((stage == RELAX) & (block > 0) & (position > 0))
            | ((stage == FINAL) & (block > 1) & (position < last))
        )

    def passes_on(stage):
        return (
            ((stage == FIRST) & (position == 0))
            | ((stage == CHAIN) & (position > 0) & (position < last))
            | ((stage == COARSE) & (block > 0) & (position == 0))
            | ((stage == RELAX) & (block > 0) & (position > 0) & ((position < last) | has_next))
            | ((stage == FINAL) & (block > 1) & (position < last - 1))
        )

    def is_state(stage):
        return (
            ((stage <= CHAIN) & (block == 0))
            | (((stage == COARSE) | (stage == RELAX)) & (block == 1))
            | ((stage == RELAX) & is_last)
            | (stage == FINAL)
        )

    def hop(stage, seq):
        target = jnp.where(
            stage <= CHAIN, CHAIN, jnp.where((stage == FINAL) | ((stage == RELAX) & is_last), FINAL, RELAX)
        )
        return pltpu.make_async_remote_copy(
            src_ref=tx.at[stage, seq], dst_ref=rx.at[target, seq],
            send_sem=send_sem.at[stage, seq], recv_sem=recv_sem.at[target, seq],
            device_id=at(device + 1), device_id_type=MESH,
        )

    def own_rows(of):
        return pl.ds(pl.multiple_of(of * rows, rows), rows)

    def give_share(seq, i):
        other = lax.rem(position + i, COARSEN)
        return pltpu.make_async_remote_copy(
            src_ref=term.at[seq, own_rows(other)], dst_ref=parts.at[seq, i - 1],
            send_sem=share_send.at[seq, i - 1], recv_sem=share_recv.at[seq],
            device_id=at(block * COARSEN + other), device_id_type=MESH,
        )

    def scatter_end(seq, i):
        return pltpu.make_async_remote_copy(
            src_ref=term.at[seq, own_rows(i)], dst_ref=parts.at[seq, 0],
            send_sem=share_send.at[seq, i], recv_sem=share_recv.at[seq],
            device_id=at(i), device_id_type=MESH,
        )

    def give_ahead(seq, i):
        other = lax.rem(position + i, COARSEN)
        return pltpu.make_async_remote_copy(
            src_ref=share.at[seq], dst_ref=rx.at[COARSE, seq, own_rows(position)],
            send_sem=ahead_send.at[seq, i], recv_sem=recv_sem.at[COARSE, seq],
            device_id=at((block + 1) * COARSEN + other), device_id_type=MESH,
        )

    def give_own(seq, i):
        other = lax.rem(position + i, COARSEN)
        return pltpu.make_async_remote_copy(
            src_ref=share.at[seq], dst_ref=gathered.at[seq, own_rows(position)],
            send_sem=own_send.at[seq, i - 1], recv_sem=own_recv.at[seq],
            device_id=at(block * COARSEN + other), device_id_type=MESH,
        )

    def landed(ref, sem):
        pltpu.make_async_copy(ref, ref, sem).wait()

    def give_back(seq):
        return pltpu.make_async_remote_copy(
            src_ref=rx.at[COARSE, seq], dst_ref=gathered.at[seq],
            send_sem=back_send.at[seq], recv_sem=own_recv.at[seq],
            device_id=at(device - COARSEN), device_id_type=MESH,
        )

    def finish(seq):
        mine = own_rows(position)

        @pl.when((block == 0) & is_last)
        def _():
            share[seq] = term[seq, mine]

        @pl.when((block == 0) & jnp.logical_not(is_last))
        def _():
            landed(parts.at[seq, 0], share_recv.at[seq])
            share[seq] = parts[seq, 0]

        @pl.when(block > 0)
        def _():
            landed(parts.at[seq], share_recv.at[seq])
            share[seq] = (term[seq, mine] + parts[seq, 0]) + (parts[seq, 1] + parts[seq, 2])

        @pl.when(has_next)
        def _():
            for i in range(COARSEN):
                give_ahead(seq, i).start()

        @pl.when(jnp.logical_not(has_next))
        def _():
            for i in range(1, COARSEN):
                give_own(seq, i).start()
            gathered[seq, mine] = share[seq]

    def turn(step, carry):
        stage, seq = step // micro, lax.rem(step, micro)

        @pl.when(active(stage))
        def _():
            @pl.when(stage > FIRST)
            def _():
                landed(rx.at[stage, seq], recv_sem.at[stage, seq])

            current = rx[stage, seq]
            change = step_size * delta(current, seq)
            moved = current + change

            @pl.when(passes_on(stage))
            def _():
                tx[stage, seq] = moved
                hop(stage, seq).start()

            @pl.when(stage == FIRST)
            def _():
                base[seq] = change

            @pl.when((stage == CHAIN) & is_last)
            def _():
                ends[seq] = moved - rx[FIRST, seq]

                @pl.when(block == 0)
                def _():
                    term[seq] = moved
                    for i in range(last):
                        scatter_end(seq, i).start()
                    finish(seq)

            @pl.when(stage == COARSE)
            def _():
                increment = change - base[seq]

                @pl.when(is_last)
                def _():
                    term[seq] = increment + (ends[seq] + current)

                @pl.when(jnp.logical_not(is_last))
                def _():
                    term[seq] = increment

                for i in range(1, COARSEN):
                    give_share(seq, i).start()
                give_back(seq).start()

                @pl.when(seq >= LAG)
                def _():
                    finish(seq - LAG)

            @pl.when(is_state(stage))
            def _():
                states[0, seq] = moved

        return carry

    lax.fori_loop(0, RELAX * micro, turn, 0)

    for seq in range(micro):
        early = (block == 0) & is_last
        if seq < micro - LAG:
            early = early | (block > 0)

        @pl.when(jnp.logical_not(early))
        def _():
            finish(seq)

    lax.fori_loop(RELAX * micro, STAGES * micro, turn, 0)

    for seq in range(micro):
        @pl.when(has_next)
        def _():
            landed(gathered.at[seq], own_recv.at[seq])

        @pl.when(jnp.logical_not(has_next))
        def _():
            landed(gathered.at[seq, pl.ds(0, last * rows)], own_recv.at[seq])

    coarse[0] = gathered[...]

    for seq in range(micro):
        for stage in range(STAGES):
            @pl.when(passes_on(stage))
            def _():
                hop(stage, seq).wait_send()

        @pl.when((block == 0) & is_last)
        def _():
            for i in range(last):
                scatter_end(seq, i).wait_send()

        @pl.when(block > 0)
        def _():
            for i in range(1, COARSEN):
                give_share(seq, i).wait_send()
            give_back(seq).wait_send()

        @pl.when(has_next)
        def _():
            for i in range(COARSEN):
                give_ahead(seq, i).wait_send()

        @pl.when(jnp.logical_not(has_next))
        def _():
            for i in range(1, COARSEN):
                give_own(seq, i).wait_send()


def solution(mesh):
    blocks = mesh.shape["depth"] // COARSEN

    def on_device(inputs, attn_in, attn_out, mlp_in, mlp_out, norm_gain, head_gain):
        whole = inputs.shape
        micro, frames, width = whole[0] * PIECES, whole[1] // PIECES, whole[2]
        rows = frames // COARSEN
        state = (micro, frames, width)
        out = jax.ShapeDtypeStruct((1,) + state, jnp.float32)
        vmem = pl.BlockSpec(memory_space=pltpu.VMEM)
        dma = pltpu.SemaphoreType.DMA
        weights = (attn_in, attn_out, mlp_in, mlp_out, norm_gain, head_gain)
        results = pl.pallas_call(
            functools.partial(kernel, blocks),
            out_shape=(out, out),
            in_specs=[pl.BlockSpec(memory_space=pl.ANY)] * 7,
            out_specs=(vmem, vmem),
            scratch_shapes=[
                *(pltpu.VMEM(weight.shape, weight.dtype) for weight in weights),
                pltpu.VMEM(whole[1:], jnp.bfloat16),
                pltpu.VMEM(whole[1:], jnp.bfloat16),
                dma((len(weights) + 1,)),
                pltpu.VMEM((STAGES,) + state, jnp.float32),
                pltpu.VMEM((STAGES,) + state, jnp.float32),
                pltpu.VMEM(state, jnp.float32),
                pltpu.VMEM(state, jnp.float32),
                pltpu.VMEM(state, jnp.float32),
                pltpu.VMEM((micro, rows, width), jnp.float32),
                pltpu.VMEM((micro, COARSEN - 1, rows, width), jnp.float32),
                pltpu.VMEM(state, jnp.float32),
                pltpu.VMEM((GROUP, GROUP), jnp.bfloat16),
                pltpu.VMEM((1, width), jnp.float32),
                pltpu.VMEM((1, width), jnp.float32),
                dma((STAGES, micro)),
                dma((STAGES, micro)),
                dma((micro, COARSEN - 1)),
                dma((micro,)),
                dma((micro, COARSEN)),
                dma((micro, COARSEN - 1)),
                dma((micro,)),
                dma((micro,)),
            ],
            compiler_params=pltpu.CompilerParams(
                collective_id=0, has_side_effects=True, vmem_limit_bytes=64_000_000
            ),
        )(inputs.reshape(state), *weights)
        return tuple(result.reshape((1,) + whole) for result in results)

    in_specs = (
        P("batch", None, None),
        P("depth", None, None),
        P("depth", None, None),
        P("depth", None, None),
        P("depth", None, None),
        P("depth", None),
        P("depth", None),
    )
    out_specs = (P("depth", "batch", None, None), P("depth", "batch", None, None))
    return jax.shard_map(
        on_device, mesh=mesh, in_specs=in_specs, out_specs=out_specs, check_vma=False
    )
```

```python
import functools
import math

import jax
import jax.numpy as jnp
from jax import lax
from jax.experimental import pallas as pl
from jax.experimental.pallas import tpu as pltpu
from jax.sharding import PartitionSpec as P

COARSEN = 4
GROUP = 256
PIECES = 2
LAG = 3

step_size = 0.25
epsilon = 1e-06

FIRST, CHAIN, COARSE, RELAX, FINAL = range(5)
STAGES = 5
MESH = pl.DeviceIdType.MESH


def kernel(
    blocks, inputs, h_qkv, h_out, h_up, h_down, h_gain, h_head, states, coarse,
    w_qkv, w_out, w_up, w_down, in_gain, qk_gain, keys_ref, values_ref, load_sem, rx, tx, base, ends, term, share, parts, gathered, same_head, head_scale, query_scale,
    send_sem, recv_sem, share_send, share_recv, ahead_send, own_send, own_recv, back_send,
):
    micro, frames, width = inputs.shape
    head_dim = qk_gain.shape[1]
    rows = frames // COARSEN
    device = lax.axis_index("depth")
    position = lax.rem(device, COARSEN)
    block = device // COARSEN
    has_next = block < blocks - 1
    last = COARSEN - 1
    is_last = position == last

    loads = [
        pltpu.make_async_copy(source, target, load_sem.at[i])
        for i, (source, target) in enumerate((
            (h_head, qk_gain), (h_gain, in_gain), (inputs, rx.at[FIRST]), (h_qkv, w_qkv),
            (h_up, w_up), (h_out, w_out), (h_down, w_down),
        ))
    ]
    for load in loads:
        load.start()

    def at(depth):
        return {"depth": depth}

    barrier = pltpu.get_barrier_semaphore()
    for i in range(COARSEN):
        @pl.when(block > 0)
        def _():
            pl.semaphore_signal(barrier, inc=1, device_id=at((block - 1) * COARSEN + i), device_id_type=MESH)

        @pl.when(has_next)
        def _():
            pl.semaphore_signal(barrier, inc=1, device_id=at((block + 1) * COARSEN + i), device_id_type=MESH)

    for i in range(1, COARSEN):
        other = block * COARSEN + lax.rem(position + i, COARSEN)
        pl.semaphore_signal(barrier, inc=1, device_id=at(other), device_id_type=MESH)

    heads_of = lax.broadcasted_iota(jnp.int32, (GROUP, GROUP), 0) // head_dim
    heads_at = lax.broadcasted_iota(jnp.int32, (GROUP, GROUP), 1) // head_dim
    same_head[...] = jnp.where(heads_of == heads_at, 1.0, 0.0).astype(jnp.bfloat16)
    keys_ref[...] = jnp.zeros_like(keys_ref)
    values_ref[...] = jnp.zeros_like(values_ref)
    loads[0].wait()
    head_scale[...] = jnp.concatenate([qk_gain[...]] * (width // head_dim), axis=1)
    query_scale[...] = head_scale[...] * (1.0 / math.sqrt(head_dim))

    neighbours = (block > 0).astype(jnp.int32) + has_next.astype(jnp.int32)
    pl.semaphore_wait(barrier, COARSEN - 1 + COARSEN * neighbours)

    for load in loads[1:]:
        load.wait()

    def delta(current, unit):
        piece = lax.rem(unit, PIECES)
        here = pl.ds(pl.multiple_of(piece * frames, frames), frames)
        spread = jnp.mean(current * current, axis=-1, keepdims=True) + epsilon
        row_scale = lax.rsqrt(spread)
        gained = (current * in_gain[...]).astype(jnp.bfloat16)
        same = same_head[...]
        copies = GROUP // head_dim
        causal = lax.broadcasted_iota(jnp.int32, (frames, GROUP), 0) + piece * frames >= lax.rem(
            lax.broadcasted_iota(jnp.int32, (frames, GROUP), 1), PIECES * frames
        )
        starts = range(0, width, GROUP)
        half = w_up.shape[2] // 2

        def project(part):
            return jnp.dot(
                gained, w_qkv[0, :, part * width:(part + 1) * width], preferred_element_type=jnp.float32
            )

        def head_norm(rows_of, scale_of):
            cut = [rows_of[:, start:start + GROUP] for start in starts]
            squares = jnp.concatenate([(part * part).astype(jnp.bfloat16) for part in cut], axis=0)
            means = jnp.dot(squares, same, preferred_element_type=jnp.float32) * (1.0 / head_dim)
            scales = lax.rsqrt(means + jnp.concatenate([epsilon * spread] * len(cut), axis=0))
            return [
                (part * (scales[i * frames:(i + 1) * frames] * scale_of[:, start:start + GROUP])).astype(jnp.bfloat16)
                for i, (part, start) in enumerate(zip(cut, starts))
            ]

        def raise_half(i):
            raised = jnp.dot(gained, w_up[0, :, i * half:(i + 1) * half], preferred_element_type=jnp.float32)
            return jax.nn.gelu(raised * row_scale, approximate=True).astype(jnp.bfloat16)

        def lower_half(i, hidden):
            return jnp.dot(hidden, w_down[0, i * half:(i + 1) * half], preferred_element_type=jnp.float32)

        key_rows = project(1)
        query_rows = project(0)
        keys_of = head_norm(key_rows, head_scale)
        queries_of = head_norm(query_rows, query_scale)
        values_of = (project(2) * row_scale).astype(jnp.bfloat16)
        hidden = raise_half(0)
        weights, mixes = [], []
        for i, start in enumerate(starts):
            part = slice(start, start + GROUP)
            keys_ref[here, part] = keys_of[i]
            values_ref[here, part] = values_of[:, part]
            keys = jnp.concatenate([keys_ref[:, part]] * copies, axis=0) * same
            scores = lax.dot_general(
                queries_of[i], keys, (((1,), (1,)), ((), ())), preferred_element_type=jnp.float32
            )
            weights.append(jnp.where(causal, jnp.exp(scores), 0.0).astype(jnp.bfloat16))
        late = raise_half(1)
        lowered = lower_half(0, hidden)
        for weight, start in zip(weights, starts):
            values = jnp.concatenate([values_ref[:, start:start + GROUP]] * copies, axis=0) * same
            mixes.append(jnp.dot(weight, values, preferred_element_type=jnp.float32))
        totals = jnp.dot(jnp.concatenate(weights, axis=0), same, preferred_element_type=jnp.float32)
        lowered = lowered + lower_half(1, late)
        contexts = [
            (mixed / totals[i * frames:(i + 1) * frames]).astype(jnp.bfloat16)
            for i, mixed in enumerate(mixes)
        ]
        context = jnp.concatenate(contexts, axis=1)
        return jnp.dot(context, w_out[0], preferred_element_type=jnp.float32) + lowered

    def active(stage):
        return (
            ((stage == FIRST) & ((block > 0) | (position == 0)))
            | ((stage == CHAIN) & (position > 0))
            | ((stage == COARSE) & (block > 0))
            | ((stage == RELAX) & (block > 0) & (position > 0))
            | ((stage == FINAL) & (block > 1) & (position < last))
        )

    def passes_on(stage):
        return (
            ((stage == FIRST) & (position == 0))
            | ((stage == CHAIN) & (position > 0) & (position < last))
            | ((stage == COARSE) & (block > 0) & (position == 0))
            | ((stage == RELAX) & (block > 0) & (position > 0) & ((position < last) | has_next))
            | ((stage == FINAL) & (block > 1) & (position < last - 1))
        )

    def is_state(stage):
        return (
            ((stage <= CHAIN) & (block == 0))
            | (((stage == COARSE) | (stage == RELAX)) & (block == 1))
            | ((stage == RELAX) & is_last)
            | (stage == FINAL)
        )

    def hop(stage, seq):
        target = jnp.where(
            stage <= CHAIN, CHAIN, jnp.where((stage == FINAL) | ((stage == RELAX) & is_last), FINAL, RELAX)
        )
        return pltpu.make_async_remote_copy(
            src_ref=tx.at[stage, seq], dst_ref=rx.at[target, seq],
            send_sem=send_sem.at[stage, seq], recv_sem=recv_sem.at[target, seq],
            device_id=at(device + 1), device_id_type=MESH,
        )

    def own_rows(of):
        return pl.ds(pl.multiple_of(of * rows, rows), rows)

    def give_share(seq, i):
        other = lax.rem(position + i, COARSEN)
        return pltpu.make_async_remote_copy(
            src_ref=term.at[seq, own_rows(other)], dst_ref=parts.at[seq, i - 1],
            send_sem=share_send.at[seq, i - 1], recv_sem=share_recv.at[seq],
            device_id=at(block * COARSEN + other), device_id_type=MESH,
        )

    def scatter_end(seq, i):
        return pltpu.make_async_remote_copy(
            src_ref=term.at[seq, own_rows(i)], dst_ref=parts.at[seq, 0],
            send_sem=share_send.at[seq, i], recv_sem=share_recv.at[seq],
            device_id=at(i), device_id_type=MESH,
        )

    def give_ahead(seq, i):
        other = lax.rem(position + i, COARSEN)
        return pltpu.make_async_remote_copy(
            src_ref=share.at[seq], dst_ref=rx.at[COARSE, seq, own_rows(position)],
            send_sem=ahead_send.at[seq, i], recv_sem=recv_sem.at[COARSE, seq],
            device_id=at((block + 1) * COARSEN + other), device_id_type=MESH,
        )

    def give_own(seq, i):
        other = lax.rem(position + i, COARSEN)
        return pltpu.make_async_remote_copy(
            src_ref=share.at[seq], dst_ref=gathered.at[seq, own_rows(position)],
            send_sem=own_send.at[seq, i - 1], recv_sem=own_recv.at[seq],
            device_id=at(block * COARSEN + other), device_id_type=MESH,
        )

    def landed(ref, sem):
        pltpu.make_async_copy(ref, ref, sem).wait()

    def give_back(seq):
        return pltpu.make_async_remote_copy(
            src_ref=rx.at[COARSE, seq], dst_ref=gathered.at[seq],
            send_sem=back_send.at[seq], recv_sem=own_recv.at[seq],
            device_id=at(device - COARSEN), device_id_type=MESH,
        )

    def finish(seq):
        mine = own_rows(position)

        @pl.when((block == 0) & is_last)
        def _():
            share[seq] = term[seq, mine]

        @pl.when((block == 0) & jnp.logical_not(is_last))
        def _():
            landed(parts.at[seq, 0], share_recv.at[seq])
            share[seq] = parts[seq, 0]

        @pl.when(block > 0)
        def _():
            landed(parts.at[seq], share_recv.at[seq])
            share[seq] = (term[seq, mine] + parts[seq, 0]) + (parts[seq, 1] + parts[seq, 2])

        @pl.when(has_next)
        def _():
            for i in range(COARSEN):
                give_ahead(seq, i).start()

        @pl.when(jnp.logical_not(has_next))
        def _():
            for i in range(1, COARSEN):
                give_own(seq, i).start()
            gathered[seq, mine] = share[seq]

    def turn(step, carry):
        stage, seq = step // micro, lax.rem(step, micro)

        @pl.when(active(stage))
        def _():
            @pl.when(stage > FIRST)
            def _():
                landed(rx.at[stage, seq], recv_sem.at[stage, seq])

            current = rx[stage, seq]
            change = step_size * delta(current, seq)
            moved = current + change

            @pl.when(passes_on(stage))
            def _():
                tx[stage, seq] = moved
                hop(stage, seq).start()

            @pl.when(stage == FIRST)
            def _():
                base[seq] = change

            @pl.when((stage == CHAIN) & is_last)
            def _():
                ends[seq] = moved - rx[FIRST, seq]

                @pl.when(block == 0)
                def _():
                    term[seq] = moved
                    for i in range(last):
                        scatter_end(seq, i).start()
                    finish(seq)

            @pl.when(stage == COARSE)
            def _():
                increment = change - base[seq]

                @pl.when(is_last)
                def _():
                    term[seq] = increment + (ends[seq] + current)

                @pl.when(jnp.logical_not(is_last))
                def _():
                    term[seq] = increment

                for i in range(1, COARSEN):
                    give_share(seq, i).start()
                give_back(seq).start()

            @pl.when(is_state(stage))
            def _():
                states[0, seq] = moved

            since = step - COARSE * micro - LAG
            turns = jnp.where(position == 1, micro, micro - LAG)

            @pl.when((block > 0) & (since >= 0) & (since < turns))
            def _():
                finish(since)

        return carry

    def finish_left(first, last_seq, when):
        for seq in range(first, last_seq):
            @pl.when(when)
            def _():
                finish(seq)

    lax.fori_loop(0, RELAX * micro, turn, 0)
    finish_left(0, micro, (block == 0) & jnp.logical_not(is_last))
    finish_left(max(micro - LAG, 0), micro, (block > 0) & (position != 1))
    lax.fori_loop(RELAX * micro, STAGES * micro, turn, 0)

    for seq in range(micro):
        @pl.when(has_next)
        def _():
            landed(gathered.at[seq], own_recv.at[seq])

        @pl.when(jnp.logical_not(has_next))
        def _():
            landed(gathered.at[seq, pl.ds(0, last * rows)], own_recv.at[seq])

    coarse[0] = gathered[...]

    for seq in range(micro):
        for stage in range(STAGES):
            @pl.when(passes_on(stage))
            def _():
                hop(stage, seq).wait_send()

        @pl.when((block == 0) & is_last)
        def _():
            for i in range(last):
                scatter_end(seq, i).wait_send()

        @pl.when(block > 0)
        def _():
            for i in range(1, COARSEN):
                give_share(seq, i).wait_send()
            give_back(seq).wait_send()

        @pl.when(has_next)
        def _():
            for i in range(COARSEN):
                give_ahead(seq, i).wait_send()

        @pl.when(jnp.logical_not(has_next))
        def _():
            for i in range(1, COARSEN):
                give_own(seq, i).wait_send()


def solution(mesh):
    blocks = mesh.shape["depth"] // COARSEN

    def on_device(inputs, attn_in, attn_out, mlp_in, mlp_out, norm_gain, head_gain):
        whole = inputs.shape
        micro, frames, width = whole[0] * PIECES, whole[1] // PIECES, whole[2]
        rows = frames // COARSEN
        state = (micro, frames, width)
        out = jax.ShapeDtypeStruct((1,) + state, jnp.float32)
        vmem = pl.BlockSpec(memory_space=pltpu.VMEM)
        dma = pltpu.SemaphoreType.DMA
        weights = (attn_in, attn_out, mlp_in, mlp_out, norm_gain, head_gain)
        results = pl.pallas_call(
            functools.partial(kernel, blocks),
            out_shape=(out, out),
            in_specs=[pl.BlockSpec(memory_space=pl.ANY)] * 7,
            out_specs=(vmem, vmem),
            scratch_shapes=[
                *(pltpu.VMEM(weight.shape, weight.dtype) for weight in weights),
                pltpu.VMEM(whole[1:], jnp.bfloat16),
                pltpu.VMEM(whole[1:], jnp.bfloat16),
                dma((len(weights) + 1,)),
                pltpu.VMEM((STAGES,) + state, jnp.float32),
                pltpu.VMEM((STAGES,) + state, jnp.float32),
                pltpu.VMEM(state, jnp.float32),
                pltpu.VMEM(state, jnp.float32),
                pltpu.VMEM(state, jnp.float32),
                pltpu.VMEM((micro, rows, width), jnp.float32),
                pltpu.VMEM((micro, COARSEN - 1, rows, width), jnp.float32),
                pltpu.VMEM(state, jnp.float32),
                pltpu.VMEM((GROUP, GROUP), jnp.bfloat16),
                pltpu.VMEM((1, width), jnp.float32),
                pltpu.VMEM((1, width), jnp.float32),
                dma((STAGES, micro)),
                dma((STAGES, micro)),
                dma((micro, COARSEN - 1)),
                dma((micro,)),
                dma((micro, COARSEN)),
                dma((micro, COARSEN - 1)),
                dma((micro,)),
                dma((micro,)),
            ],
            compiler_params=pltpu.CompilerParams(
                collective_id=0, has_side_effects=True, vmem_limit_bytes=56_000_000
            ),
        )(inputs.reshape(state), *weights)
        return tuple(result.reshape((1,) + whole) for result in results)

    in_specs = (
        P("batch", None, None),
        P("depth", None, None),
        P("depth", None, None),
        P("depth", None, None),
        P("depth", None, None),
        P("depth", None),
        P("depth", None),
    )
    out_specs = (P("depth", "batch", None, None), P("depth", "batch", None, None))
    return jax.shard_map(
        on_device, mesh=mesh, in_specs=in_specs, out_specs=out_specs, check_vma=False
    )
```

```python
import functools
import math

import jax
import jax.numpy as jnp
from jax import lax
from jax.experimental import pallas as pl
from jax.experimental.pallas import tpu as pltpu
from jax.sharding import PartitionSpec as P

COARSEN = 4
GROUP = 256
PIECES = 2
LAG = 3

step_size = 0.25
epsilon = 1e-06

FIRST, CHAIN, COARSE, RELAX, FINAL = range(5)
STAGES = 5
MESH = pl.DeviceIdType.MESH


def kernel(
    blocks, inputs, h_qkv, h_out, h_up, h_down, h_gain, h_head, states, coarse,
    w_qkv, w_out, w_up, w_down, in_gain, qk_gain, keys_ref, values_ref, load_sem, rx, tx, base, ends, term, share, parts, gathered, same_head, head_scale, query_scale,
    send_sem, recv_sem, share_send, share_recv, ahead_send, own_send, own_recv, back_send,
):
    micro, frames, width = inputs.shape
    head_dim = qk_gain.shape[1]
    rows = frames // COARSEN
    device = lax.axis_index("depth")
    position = lax.rem(device, COARSEN)
    block = device // COARSEN
    has_next = block < blocks - 1
    last = COARSEN - 1
    is_last = position == last

    def columns(ref, part):
        return ref.at[0, :, pl.ds(part * width, width)]

    loads = [
        pltpu.make_async_copy(source, target, load_sem.at[i])
        for i, (source, target) in enumerate((
            (h_head, qk_gain), (h_gain, in_gain), (inputs, rx.at[FIRST]),
            *((columns(h_qkv, part), columns(w_qkv, part)) for part in (1, 0, 2)),
            (h_up, w_up), (h_down, w_down), (h_out, w_out),
        ))
    ]
    load_keys, load_queries, load_values, load_up, load_down, load_out = loads[3:]
    for load in loads:
        load.start()

    def at(depth):
        return {"depth": depth}

    barrier = pltpu.get_barrier_semaphore()
    for i in range(COARSEN):
        @pl.when(block > 0)
        def _():
            pl.semaphore_signal(barrier, inc=1, device_id=at((block - 1) * COARSEN + i), device_id_type=MESH)

        @pl.when(has_next)
        def _():
            pl.semaphore_signal(barrier, inc=1, device_id=at((block + 1) * COARSEN + i), device_id_type=MESH)

    for i in range(1, COARSEN):
        other = block * COARSEN + lax.rem(position + i, COARSEN)
        pl.semaphore_signal(barrier, inc=1, device_id=at(other), device_id_type=MESH)

    heads_of = lax.broadcasted_iota(jnp.int32, (GROUP, GROUP), 0) // head_dim
    heads_at = lax.broadcasted_iota(jnp.int32, (GROUP, GROUP), 1) // head_dim
    same_head[...] = jnp.where(heads_of == heads_at, 1.0, 0.0).astype(jnp.bfloat16)
    keys_ref[...] = jnp.zeros_like(keys_ref)
    values_ref[...] = jnp.zeros_like(values_ref)
    loads[0].wait()
    head_scale[...] = jnp.concatenate([qk_gain[...]] * (width // head_dim), axis=1)
    query_scale[...] = head_scale[...] * (1.0 / math.sqrt(head_dim))

    neighbours = (block > 0).astype(jnp.int32) + has_next.astype(jnp.int32)
    loads[1].wait()
    loads[2].wait()

    def keep(value, load):
        return value

    def fetched(value, load):
        load.wait()
        return value

    def delta(current, unit, after=keep):
        piece = lax.rem(unit, PIECES)
        here = pl.ds(pl.multiple_of(piece * frames, frames), frames)
        spread = jnp.mean(current * current, axis=-1, keepdims=True) + epsilon
        row_scale = lax.rsqrt(spread)
        gained = (current * in_gain[...]).astype(jnp.bfloat16)
        same = same_head[...]
        copies = GROUP // head_dim
        causal = lax.broadcasted_iota(jnp.int32, (frames, GROUP), 0) + piece * frames >= lax.rem(
            lax.broadcasted_iota(jnp.int32, (frames, GROUP), 1), PIECES * frames
        )
        starts = range(0, width, GROUP)
        half = w_up.shape[2] // 2

        def project(part, load):
            return jnp.dot(
                after(gained, load), w_qkv[0, :, part * width:(part + 1) * width], preferred_element_type=jnp.float32
            )

        def head_norm(rows_of, scale_of):
            cut = [rows_of[:, start:start + GROUP] for start in starts]
            squares = jnp.concatenate([(part * part).astype(jnp.bfloat16) for part in cut], axis=0)
            means = jnp.dot(squares, same, preferred_element_type=jnp.float32) * (1.0 / head_dim)
            scales = lax.rsqrt(means + jnp.concatenate([epsilon * spread] * len(cut), axis=0))
            return [
                (part * (scales[i * frames:(i + 1) * frames] * scale_of[:, start:start + GROUP])).astype(jnp.bfloat16)
                for i, (part, start) in enumerate(zip(cut, starts))
            ]

        def raise_half(i):
            raised = jnp.dot(gained, w_up[0, :, i * half:(i + 1) * half], preferred_element_type=jnp.float32)
            return jax.nn.gelu(raised * row_scale, approximate=True).astype(jnp.bfloat16)

        def lower_half(i, hidden):
            return jnp.dot(hidden, w_down[0, i * half:(i + 1) * half], preferred_element_type=jnp.float32)

        key_rows = project(1, load_keys)
        query_rows = project(0, load_queries)
        keys_of = head_norm(key_rows, head_scale)
        queries_of = head_norm(query_rows, query_scale)
        values_of = (project(2, load_values) * row_scale).astype(jnp.bfloat16)
        after(gained, load_up)
        hidden = raise_half(0)
        weights, mixes = [], []
        for i, start in enumerate(starts):
            part = slice(start, start + GROUP)
            keys_ref[here, part] = keys_of[i]
            values_ref[here, part] = values_of[:, part]
            keys = jnp.concatenate([keys_ref[:, part]] * copies, axis=0) * same
            scores = lax.dot_general(
                queries_of[i], keys, (((1,), (1,)), ((), ())), preferred_element_type=jnp.float32
            )
            weights.append(jnp.where(causal, jnp.exp(scores), 0.0).astype(jnp.bfloat16))
        late = raise_half(1)
        after(hidden, load_down)
        lowered = lower_half(0, hidden)
        for weight, start in zip(weights, starts):
            values = jnp.concatenate([values_ref[:, start:start + GROUP]] * copies, axis=0) * same
            mixes.append(jnp.dot(weight, values, preferred_element_type=jnp.float32))
        totals = jnp.dot(jnp.concatenate(weights, axis=0), same, preferred_element_type=jnp.float32)
        lowered = lowered + lower_half(1, late)
        contexts = [
            (mixed / totals[i * frames:(i + 1) * frames]).astype(jnp.bfloat16)
            for i, mixed in enumerate(mixes)
        ]
        context = jnp.concatenate(contexts, axis=1)
        after(context, load_out)
        return jnp.dot(context, w_out[0], preferred_element_type=jnp.float32) + lowered

    def active(stage):
        return (
            ((stage == FIRST) & ((block > 0) | (position == 0)))
            | ((stage == CHAIN) & (position > 0))
            | ((stage == COARSE) & (block > 0))
            | ((stage == RELAX) & (block > 0) & (position > 0))
            | ((stage == FINAL) & (block > 1) & (position < last))
        )

    def passes_on(stage):
        return (
            ((stage == FIRST) & (position == 0))
            | ((stage == CHAIN) & (position > 0) & (position < last))
            | ((stage == COARSE) & (block > 0) & (position == 0))
            | ((stage == RELAX) & (block > 0) & (position > 0) & ((position < last) | has_next))
            | ((stage == FINAL) & (block > 1) & (position < last - 1))
        )

    def is_state(stage):
        return (
            ((stage <= CHAIN) & (block == 0))
            | (((stage == COARSE) | (stage == RELAX)) & (block == 1))
            | ((stage == RELAX) & is_last)
            | (stage == FINAL)
        )

    def hop(stage, seq):
        target = jnp.where(
            stage <= CHAIN, CHAIN, jnp.where((stage == FINAL) | ((stage == RELAX) & is_last), FINAL, RELAX)
        )
        return pltpu.make_async_remote_copy(
            src_ref=tx.at[stage, seq], dst_ref=rx.at[target, seq],
            send_sem=send_sem.at[stage, seq], recv_sem=recv_sem.at[target, seq],
            device_id=at(device + 1), device_id_type=MESH,
        )

    def own_rows(of):
        return pl.ds(pl.multiple_of(of * rows, rows), rows)

    def give_share(seq, i):
        other = lax.rem(position + i, COARSEN)
        return pltpu.make_async_remote_copy(
            src_ref=term.at[seq, own_rows(other)], dst_ref=parts.at[seq, i - 1],
            send_sem=share_send.at[seq, i - 1], recv_sem=share_recv.at[seq],
            device_id=at(block * COARSEN + other), device_id_type=MESH,
        )

    def scatter_end(seq, i):
        return pltpu.make_async_remote_copy(
            src_ref=term.at[seq, own_rows(i)], dst_ref=parts.at[seq, 0],
            send_sem=share_send.at[seq, i], recv_sem=share_recv.at[seq],
            device_id=at(i), device_id_type=MESH,
        )

    def give_ahead(seq, i):
        other = lax.rem(position + i, COARSEN)
        return pltpu.make_async_remote_copy(
            src_ref=share.at[seq], dst_ref=rx.at[COARSE, seq, own_rows(position)],
            send_sem=ahead_send.at[seq, i], recv_sem=recv_sem.at[COARSE, seq],
            device_id=at((block + 1) * COARSEN + other), device_id_type=MESH,
        )

    def give_own(seq, i):
        other = lax.rem(position + i, COARSEN)
        return pltpu.make_async_remote_copy(
            src_ref=share.at[seq], dst_ref=gathered.at[seq, own_rows(position)],
            send_sem=own_send.at[seq, i - 1], recv_sem=own_recv.at[seq],
            device_id=at(block * COARSEN + other), device_id_type=MESH,
        )

    def landed(ref, sem):
        pltpu.make_async_copy(ref, ref, sem).wait()

    def give_back(seq):
        return pltpu.make_async_remote_copy(
            src_ref=rx.at[COARSE, seq], dst_ref=gathered.at[seq],
            send_sem=back_send.at[seq], recv_sem=own_recv.at[seq],
            device_id=at(device - COARSEN), device_id_type=MESH,
        )

    def finish(seq):
        mine = own_rows(position)

        @pl.when((block == 0) & is_last)
        def _():
            share[seq] = term[seq, mine]

        @pl.when((block == 0) & jnp.logical_not(is_last))
        def _():
            landed(parts.at[seq, 0], share_recv.at[seq])
            share[seq] = parts[seq, 0]

        @pl.when(block > 0)
        def _():
            landed(parts.at[seq], share_recv.at[seq])
            share[seq] = (term[seq, mine] + parts[seq, 0]) + (parts[seq, 1] + parts[seq, 2])

        @pl.when(has_next)
        def _():
            for i in range(COARSEN):
                give_ahead(seq, i).start()

        @pl.when(jnp.logical_not(has_next))
        def _():
            for i in range(1, COARSEN):
                give_own(seq, i).start()
            gathered[seq, mine] = share[seq]

    def turn(step, carry):
        stage, seq = step // micro, lax.rem(step, micro)

        @pl.when(active(stage))
        def _():
            @pl.when(stage > FIRST)
            def _():
                landed(rx.at[stage, seq], recv_sem.at[stage, seq])

            current = rx[stage, seq]
            change = step_size * delta(current, seq)
            moved = current + change

            @pl.when(passes_on(stage))
            def _():
                tx[stage, seq] = moved
                hop(stage, seq).start()

            @pl.when(stage == FIRST)
            def _():
                base[seq] = change

            @pl.when((stage == CHAIN) & is_last)
            def _():
                ends[seq] = moved - rx[FIRST, seq]

                @pl.when(block == 0)
                def _():
                    term[seq] = moved
                    for i in range(last):
                        scatter_end(seq, i).start()
                    finish(seq)

            @pl.when(stage == COARSE)
            def _():
                increment = change - base[seq]

                @pl.when(is_last)
                def _():
                    term[seq] = increment + (ends[seq] + current)

                @pl.when(jnp.logical_not(is_last))
                def _():
                    term[seq] = increment

                for i in range(1, COARSEN):
                    give_share(seq, i).start()
                give_back(seq).start()

            @pl.when(is_state(stage))
            def _():
                states[0, seq] = moved

            since = step - COARSE * micro - LAG
            turns = jnp.where(position == 1, micro, micro - LAG)

            @pl.when((block > 0) & (since >= 0) & (since < turns))
            def _():
                finish(since)

        return carry

    def finish_left(first, last_seq, when):
        for seq in range(first, last_seq):
            @pl.when(when)
            def _():
                finish(seq)

    current = rx[FIRST, 0]
    change = step_size * delta(current, 0, fetched)
    base[0] = change
    pl.semaphore_wait(barrier, COARSEN - 1 + COARSEN * neighbours)
    moved = current + change

    @pl.when(position == 0)
    def _():
        tx[FIRST, 0] = moved
        hop(FIRST, 0).start()

    @pl.when(block == 0)
    def _():
        states[0, 0] = moved

    lax.fori_loop(1, RELAX * micro, turn, 0)
    finish_left(0, micro, (block == 0) & jnp.logical_not(is_last))
    finish_left(max(micro - LAG, 0), micro, (block > 0) & (position != 1))
    lax.fori_loop(RELAX * micro, STAGES * micro, turn, 0)

    for seq in range(micro):
        @pl.when(has_next)
        def _():
            landed(gathered.at[seq], own_recv.at[seq])

        @pl.when(jnp.logical_not(has_next))
        def _():
            landed(gathered.at[seq, pl.ds(0, last * rows)], own_recv.at[seq])

    coarse[0] = gathered[...]

    for seq in range(micro):
        for stage in range(STAGES):
            @pl.when(passes_on(stage))
            def _():
                hop(stage, seq).wait_send()

        @pl.when((block == 0) & is_last)
        def _():
            for i in range(last):
                scatter_end(seq, i).wait_send()

        @pl.when(block > 0)
        def _():
            for i in range(1, COARSEN):
                give_share(seq, i).wait_send()
            give_back(seq).wait_send()

        @pl.when(has_next)
        def _():
            for i in range(COARSEN):
                give_ahead(seq, i).wait_send()

        @pl.when(jnp.logical_not(has_next))
        def _():
            for i in range(1, COARSEN):
                give_own(seq, i).wait_send()


def hand_over(states, coarse, states_out, coarse_out, sem):
    copies = [
        pltpu.make_async_copy(source, target, sem.at[i])
        for i, (source, target) in enumerate(((states, states_out), (coarse, coarse_out)))
    ]
    for copy in copies:
        copy.start()
    for copy in copies:
        copy.wait()


def solution(mesh):
    blocks = mesh.shape["depth"] // COARSEN

    def on_device(inputs, attn_in, attn_out, mlp_in, mlp_out, norm_gain, head_gain):
        whole = inputs.shape
        micro, frames, width = whole[0] * PIECES, whole[1] // PIECES, whole[2]
        rows = frames // COARSEN
        state = (micro, frames, width)
        out = jax.ShapeDtypeStruct((1,) + state, jnp.float32)
        vmem = pl.BlockSpec(memory_space=pltpu.VMEM)
        dma = pltpu.SemaphoreType.DMA
        weights = (attn_in, attn_out, mlp_in, mlp_out, norm_gain, head_gain)
        results = pl.pallas_call(
            functools.partial(kernel, blocks),
            out_shape=(out, out),
            in_specs=[pl.BlockSpec(memory_space=pl.ANY)] * 7,
            out_specs=(vmem, vmem),
            scratch_shapes=[
                *(pltpu.VMEM(weight.shape, weight.dtype) for weight in weights),
                pltpu.VMEM(whole[1:], jnp.bfloat16),
                pltpu.VMEM(whole[1:], jnp.bfloat16),
                dma((len(weights) + 3,)),
                pltpu.VMEM((STAGES,) + state, jnp.float32),
                pltpu.VMEM((STAGES,) + state, jnp.float32),
                pltpu.VMEM(state, jnp.float32),
                pltpu.VMEM(state, jnp.float32),
                pltpu.VMEM(state, jnp.float32),
                pltpu.VMEM((micro, rows, width), jnp.float32),
                pltpu.VMEM((micro, COARSEN - 1, rows, width), jnp.float32),
                pltpu.VMEM(state, jnp.float32),
                pltpu.VMEM((GROUP, GROUP), jnp.bfloat16),
                pltpu.VMEM((1, width), jnp.float32),
                pltpu.VMEM((1, width), jnp.float32),
                dma((STAGES, micro)),
                dma((STAGES, micro)),
                dma((micro, COARSEN - 1)),
                dma((micro,)),
                dma((micro, COARSEN)),
                dma((micro, COARSEN - 1)),
                dma((micro,)),
                dma((micro,)),
            ],
            compiler_params=pltpu.CompilerParams(
                collective_id=0, has_side_effects=True, vmem_limit_bytes=56_000_000
            ),
        )(*(pltpu.with_memory_space_constraint(v, pltpu.HBM) for v in (inputs.reshape(state), *weights)))
        return pl.pallas_call(
            hand_over,
            out_shape=(jax.ShapeDtypeStruct((1,) + whole, jnp.float32),) * 2,
            in_specs=[pl.BlockSpec(memory_space=pl.ANY)] * 2,
            out_specs=(pl.BlockSpec(memory_space=pltpu.HBM),) * 2,
            scratch_shapes=[dma((2,))],
            compiler_params=pltpu.CompilerParams(vmem_limit_bytes=1_000_000),
        )(*(result.reshape((1,) + whole) for result in results))

    in_specs = (
        P("batch", None, None),
        P("depth", None, None),
        P("depth", None, None),
        P("depth", None, None),
        P("depth", None, None),
        P("depth", None),
        P("depth", None),
    )
    out_specs = (P("depth", "batch", None, None), P("depth", "batch", None, None))
    return jax.shard_map(
        on_device, mesh=mesh, in_specs=in_specs, out_specs=out_specs, check_vma=False
    )
```

```python
import functools
import math

import jax
import jax.numpy as jnp
from jax import lax
from jax.experimental import pallas as pl
from jax.experimental.pallas import tpu as pltpu
from jax.sharding import PartitionSpec as P

COARSEN = 4
GROUP = 256
PIECES = 2
LAG = 3

step_size = 0.25
epsilon = 1e-06

FIRST, CHAIN, COARSE, RELAX, FINAL = range(5)
STAGES = 5
MESH = pl.DeviceIdType.MESH


def kernel(
    blocks, inputs, h_qkv, h_out, h_up, h_down, h_gain, h_head, states, coarse,
    w_qkv, w_out, w_up, w_down, in_gain, qk_gain, keys_ref, values_ref, load_sem, rx, tx, base, ends, term, share, parts, gathered, same_head, head_scale, query_scale,
    send_sem, recv_sem, share_send, share_recv, ahead_send, own_send, own_recv, back_send,
):
    micro, frames, width = inputs.shape
    head_dim = qk_gain.shape[1]
    rows = frames // COARSEN
    device = lax.axis_index("depth")
    position = lax.rem(device, COARSEN)
    block = device // COARSEN
    has_next = block < blocks - 1
    last = COARSEN - 1
    is_last = position == last

    def columns(ref, part):
        return ref.at[0, :, pl.ds(part * width, width)]

    loads = [
        pltpu.make_async_copy(source, target, load_sem.at[i])
        for i, (source, target) in enumerate((
            (h_head, qk_gain), (h_gain, in_gain), (inputs, rx.at[FIRST]),
            *((columns(h_qkv, part), columns(w_qkv, part)) for part in (1, 0, 2)),
            (h_up, w_up), (h_down, w_down), (h_out, w_out),
        ))
    ]
    load_keys, load_queries, load_values, load_up, load_down, load_out = loads[3:]
    for load in loads:
        load.start()

    def at(depth):
        return {"depth": depth}

    barrier = pltpu.get_barrier_semaphore()
    for i in range(COARSEN):
        @pl.when(block > 0)
        def _():
            pl.semaphore_signal(barrier, inc=1, device_id=at((block - 1) * COARSEN + i), device_id_type=MESH)

        @pl.when(has_next)
        def _():
            pl.semaphore_signal(barrier, inc=1, device_id=at((block + 1) * COARSEN + i), device_id_type=MESH)

    for i in range(1, COARSEN):
        other = block * COARSEN + lax.rem(position + i, COARSEN)
        pl.semaphore_signal(barrier, inc=1, device_id=at(other), device_id_type=MESH)

    heads_of = lax.broadcasted_iota(jnp.int32, (GROUP, GROUP), 0) // head_dim
    heads_at = lax.broadcasted_iota(jnp.int32, (GROUP, GROUP), 1) // head_dim
    same_head[...] = jnp.where(heads_of == heads_at, 1.0, 0.0).astype(jnp.bfloat16)
    keys_ref[...] = jnp.zeros_like(keys_ref)
    values_ref[...] = jnp.zeros_like(values_ref)
    loads[0].wait()
    head_scale[...] = jnp.concatenate([qk_gain[...]] * (width // head_dim), axis=1)
    query_scale[...] = head_scale[...] * (1.0 / math.sqrt(head_dim))

    neighbours = (block > 0).astype(jnp.int32) + has_next.astype(jnp.int32)
    loads[1].wait()
    loads[2].wait()

    def keep(value, load):
        return value

    def fetched(value, load):
        load.wait()
        return value

    def delta(current, unit, after=keep):
        piece = lax.rem(unit, PIECES)
        here = pl.ds(pl.multiple_of(piece * frames, frames), frames)
        spread = jnp.mean(current * current, axis=-1, keepdims=True) + epsilon
        row_scale = lax.rsqrt(spread)
        gained = (current * in_gain[...]).astype(jnp.bfloat16)
        same = same_head[...]
        copies = GROUP // head_dim
        causal = lax.broadcasted_iota(jnp.int32, (frames, GROUP), 0) + piece * frames >= lax.rem(
            lax.broadcasted_iota(jnp.int32, (frames, GROUP), 1), PIECES * frames
        )
        starts = range(0, width, GROUP)
        half = w_up.shape[2] // 2

        def project(part, load):
            return jnp.dot(
                after(gained, load), w_qkv[0, :, part * width:(part + 1) * width], preferred_element_type=jnp.float32
            )

        def head_norm(rows_of, scale_of):
            cut = [rows_of[:, start:start + GROUP] for start in starts]
            squares = jnp.concatenate([(part * part).astype(jnp.bfloat16) for part in cut], axis=0)
            means = jnp.dot(squares, same, preferred_element_type=jnp.float32) * (1.0 / head_dim)
            scales = lax.rsqrt(means + jnp.concatenate([epsilon * spread] * len(cut), axis=0))
            return [
                (part * (scales[i * frames:(i + 1) * frames] * scale_of[:, start:start + GROUP])).astype(jnp.bfloat16)
                for i, (part, start) in enumerate(zip(cut, starts))
            ]

        def raise_half(i):
            raised = jnp.dot(gained, w_up[0, :, i * half:(i + 1) * half], preferred_element_type=jnp.float32)
            return jax.nn.gelu(raised * row_scale, approximate=True).astype(jnp.bfloat16)

        key_rows = project(1, load_keys)
        query_rows = project(0, load_queries)
        keys_of = head_norm(key_rows, head_scale)
        queries_of = head_norm(query_rows, query_scale)
        values_of = (project(2, load_values) * row_scale).astype(jnp.bfloat16)
        after(gained, load_up)
        hidden = raise_half(0)
        weights, mixes = [], []
        for i, start in enumerate(starts):
            part = slice(start, start + GROUP)
            keys_ref[here, part] = keys_of[i]
            values_ref[here, part] = values_of[:, part]
            keys = jnp.concatenate([keys_ref[:, part]] * copies, axis=0) * same
            scores = lax.dot_general(
                queries_of[i], keys, (((1,), (1,)), ((), ())), preferred_element_type=jnp.float32
            )
            weights.append(jnp.where(causal, jnp.exp(scores), 0.0).astype(jnp.bfloat16))
        hidden = jnp.concatenate([hidden, raise_half(1)], axis=1)
        for weight, start in zip(weights, starts):
            values = jnp.concatenate([values_ref[:, start:start + GROUP]] * copies, axis=0) * same
            mixes.append(jnp.dot(weight, values, preferred_element_type=jnp.float32))
        totals = jnp.dot(jnp.concatenate(weights, axis=0), same, preferred_element_type=jnp.float32)
        after(hidden, load_down)
        lowered = jnp.dot(hidden, w_down[0], preferred_element_type=jnp.float32)
        contexts = [
            (mixed / totals[i * frames:(i + 1) * frames]).astype(jnp.bfloat16)
            for i, mixed in enumerate(mixes)
        ]
        context = jnp.concatenate(contexts, axis=1)
        after(context, load_out)
        return jnp.dot(context, w_out[0], preferred_element_type=jnp.float32) + lowered

    def active(stage):
        return (
            ((stage == FIRST) & ((block > 0) | (position == 0)))
            | ((stage == CHAIN) & (position > 0))
            | ((stage == COARSE) & (block > 0))
            | ((stage == RELAX) & (block > 0) & (position > 0))
            | ((stage == FINAL) & (block > 1) & (position < last))
        )

    def passes_on(stage):
        return (
            ((stage == FIRST) & (position == 0))
            | ((stage == CHAIN) & (position > 0) & (position < last))
            | ((stage == COARSE) & (block > 0) & (position == 0))
            | ((stage == RELAX) & (block > 0) & (position > 0) & ((position < last) | has_next))
            | ((stage == FINAL) & (block > 1) & (position < last - 1))
        )

    def is_state(stage):
        return (
            ((stage <= CHAIN) & (block == 0))
            | (((stage == COARSE) | (stage == RELAX)) & (block == 1))
            | ((stage == RELAX) & is_last)
            | (stage == FINAL)
        )

    def hop(stage, seq):
        target = jnp.where(
            stage <= CHAIN, CHAIN, jnp.where((stage == FINAL) | ((stage == RELAX) & is_last), FINAL, RELAX)
        )
        return pltpu.make_async_remote_copy(
            src_ref=tx.at[stage, seq], dst_ref=rx.at[target, seq],
            send_sem=send_sem.at[stage, seq], recv_sem=recv_sem.at[target, seq],
            device_id=at(device + 1), device_id_type=MESH,
        )

    def own_rows(of):
        return pl.ds(pl.multiple_of(of * rows, rows), rows)

    def far_first(i):
        far = last - position
        return (far, lax.rem(position + 2, COARSEN), lax.rem(far + 2, COARSEN), position)[i]

    def give_share(seq, i):
        other = far_first(i - 1)
        return pltpu.make_async_remote_copy(
            src_ref=term.at[seq, own_rows(other)], dst_ref=parts.at[seq, i - 1],
            send_sem=share_send.at[seq, i - 1], recv_sem=share_recv.at[seq],
            device_id=at(block * COARSEN + other), device_id_type=MESH,
        )

    def scatter_end(seq, i):
        return pltpu.make_async_remote_copy(
            src_ref=term.at[seq, own_rows(i)], dst_ref=parts.at[seq, 0],
            send_sem=share_send.at[seq, i], recv_sem=share_recv.at[seq],
            device_id=at(i), device_id_type=MESH,
        )

    def give_ahead(seq, i):
        other = far_first(i)
        return pltpu.make_async_remote_copy(
            src_ref=share.at[seq], dst_ref=rx.at[COARSE, seq, own_rows(position)],
            send_sem=ahead_send.at[seq, i], recv_sem=recv_sem.at[COARSE, seq],
            device_id=at((block + 1) * COARSEN + other), device_id_type=MESH,
        )

    def give_own(seq, i):
        other = far_first(i - 1)
        return pltpu.make_async_remote_copy(
            src_ref=share.at[seq], dst_ref=gathered.at[seq, own_rows(position)],
            send_sem=own_send.at[seq, i - 1], recv_sem=own_recv.at[seq],
            device_id=at(block * COARSEN + other), device_id_type=MESH,
        )

    def landed(ref, sem):
        pltpu.make_async_copy(ref, ref, sem).wait()

    def give_back(seq):
        return pltpu.make_async_remote_copy(
            src_ref=rx.at[COARSE, seq], dst_ref=gathered.at[seq],
            send_sem=back_send.at[seq], recv_sem=own_recv.at[seq],
            device_id=at(device - COARSEN), device_id_type=MESH,
        )

    def finish(seq):
        mine = own_rows(position)

        @pl.when((block == 0) & is_last)
        def _():
            share[seq] = term[seq, mine]

        @pl.when((block == 0) & jnp.logical_not(is_last))
        def _():
            landed(parts.at[seq, 0], share_recv.at[seq])
            share[seq] = parts[seq, 0]

        @pl.when(block > 0)
        def _():
            landed(parts.at[seq], share_recv.at[seq])
            share[seq] = (term[seq, mine] + parts[seq, 0]) + (parts[seq, 1] + parts[seq, 2])

        @pl.when(has_next)
        def _():
            for i in range(COARSEN):
                give_ahead(seq, i).start()

        @pl.when(jnp.logical_not(has_next))
        def _():
            for i in range(1, COARSEN):
                give_own(seq, i).start()
            gathered[seq, mine] = share[seq]

    def turn(step, carry):
        stage, seq = step // micro, lax.rem(step, micro)

        @pl.when(active(stage))
        def _():
            @pl.when(stage > FIRST)
            def _():
                landed(rx.at[stage, seq], recv_sem.at[stage, seq])

            current = rx[stage, seq]
            change = step_size * delta(current, seq)
            moved = current + change

            shares_first = (stage == COARSE) & (block == 1)

            @pl.when(passes_on(stage) & jnp.logical_not(shares_first))
            def _():
                tx[stage, seq] = moved
                hop(stage, seq).start()

            @pl.when(stage == FIRST)
            def _():
                base[seq] = change

            @pl.when((stage == CHAIN) & is_last)
            def _():
                ends[seq] = moved - rx[FIRST, seq]

                @pl.when(block == 0)
                def _():
                    term[seq] = moved
                    for i in range(last):
                        scatter_end(seq, i).start()
                    finish(seq)

            @pl.when(stage == COARSE)
            def _():
                increment = change - base[seq]

                @pl.when(is_last)
                def _():
                    term[seq] = increment + (ends[seq] + current)

                @pl.when(jnp.logical_not(is_last))
                def _():
                    term[seq] = increment

                for i in range(1, COARSEN):
                    give_share(seq, i).start()

                @pl.when(passes_on(stage) & shares_first)
                def _():
                    tx[stage, seq] = moved
                    hop(stage, seq).start()

                give_back(seq).start()

            @pl.when(is_state(stage))
            def _():
                states[0, seq] = moved

            since = step - COARSE * micro - LAG
            turns = jnp.where((position == 1) & (block > 1), micro, micro - LAG)

            @pl.when((block > 0) & (since >= 0) & (since < turns))
            def _():
                finish(since)

        return carry

    def finish_left(first, last_seq, when):
        for seq in range(first, last_seq):
            @pl.when(when)
            def _():
                finish(seq)

    current = rx[FIRST, 0]
    change = step_size * delta(current, 0, fetched)
    base[0] = change
    pl.semaphore_wait(barrier, COARSEN - 1 + COARSEN * neighbours)
    moved = current + change

    @pl.when(position == 0)
    def _():
        tx[FIRST, 0] = moved
        hop(FIRST, 0).start()

    @pl.when(block == 0)
    def _():
        states[0, 0] = moved

    lax.fori_loop(1, RELAX * micro, turn, 0)
    finish_left(0, micro, (block == 0) & jnp.logical_not(is_last))
    finish_left(max(micro - LAG, 0), micro, (block == 1) | ((block > 1) & (position != 1)))
    lax.fori_loop(RELAX * micro, STAGES * micro, turn, 0)

    for seq in range(micro):
        @pl.when(has_next)
        def _():
            landed(gathered.at[seq], own_recv.at[seq])

        @pl.when(jnp.logical_not(has_next))
        def _():
            landed(gathered.at[seq, pl.ds(0, last * rows)], own_recv.at[seq])

    coarse[0] = gathered[...]

    for seq in range(micro):
        for stage in range(STAGES):
            @pl.when(passes_on(stage))
            def _():
                hop(stage, seq).wait_send()

        @pl.when((block == 0) & is_last)
        def _():
            for i in range(last):
                scatter_end(seq, i).wait_send()

        @pl.when(block > 0)
        def _():
            for i in range(1, COARSEN):
                give_share(seq, i).wait_send()
            give_back(seq).wait_send()

        @pl.when(has_next)
        def _():
            for i in range(COARSEN):
                give_ahead(seq, i).wait_send()

        @pl.when(jnp.logical_not(has_next))
        def _():
            for i in range(1, COARSEN):
                give_own(seq, i).wait_send()


def hand_over(states, coarse, states_out, coarse_out, sem):
    copies = [
        pltpu.make_async_copy(source, target, sem.at[i])
        for i, (source, target) in enumerate(((states, states_out), (coarse, coarse_out)))
    ]
    for copy in copies:
        copy.start()
    for copy in copies:
        copy.wait()


def solution(mesh):
    blocks = mesh.shape["depth"] // COARSEN

    def on_device(inputs, attn_in, attn_out, mlp_in, mlp_out, norm_gain, head_gain):
        whole = inputs.shape
        micro, frames, width = whole[0] * PIECES, whole[1] // PIECES, whole[2]
        rows = frames // COARSEN
        state = (micro, frames, width)
        out = jax.ShapeDtypeStruct((1,) + state, jnp.float32)
        vmem = pl.BlockSpec(memory_space=pltpu.VMEM)
        dma = pltpu.SemaphoreType.DMA
        weights = (attn_in, attn_out, mlp_in, mlp_out, norm_gain, head_gain)
        results = pl.pallas_call(
            functools.partial(kernel, blocks),
            out_shape=(out, out),
            in_specs=[pl.BlockSpec(memory_space=pl.ANY)] * 7,
            out_specs=(vmem, vmem),
            scratch_shapes=[
                *(pltpu.VMEM(weight.shape, weight.dtype) for weight in weights),
                pltpu.VMEM(whole[1:], jnp.bfloat16),
                pltpu.VMEM(whole[1:], jnp.bfloat16),
                dma((len(weights) + 3,)),
                pltpu.VMEM((STAGES,) + state, jnp.float32),
                pltpu.VMEM((STAGES,) + state, jnp.float32),
                pltpu.VMEM(state, jnp.float32),
                pltpu.VMEM(state, jnp.float32),
                pltpu.VMEM(state, jnp.float32),
                pltpu.VMEM((micro, rows, width), jnp.float32),
                pltpu.VMEM((micro, COARSEN - 1, rows, width), jnp.float32),
                pltpu.VMEM(state, jnp.float32),
                pltpu.VMEM((GROUP, GROUP), jnp.bfloat16),
                pltpu.VMEM((1, width), jnp.float32),
                pltpu.VMEM((1, width), jnp.float32),
                dma((STAGES, micro)),
                dma((STAGES, micro)),
                dma((micro, COARSEN - 1)),
                dma((micro,)),
                dma((micro, COARSEN)),
                dma((micro, COARSEN - 1)),
                dma((micro,)),
                dma((micro,)),
            ],
            compiler_params=pltpu.CompilerParams(
                collective_id=0, has_side_effects=True, vmem_limit_bytes=56_000_000,
            ),
        )(*(pltpu.with_memory_space_constraint(v, pltpu.HBM) for v in (inputs.reshape(state), *weights)))
        return pl.pallas_call(
            hand_over,
            out_shape=(jax.ShapeDtypeStruct((1,) + whole, jnp.float32),) * 2,
            in_specs=[pl.BlockSpec(memory_space=pl.ANY)] * 2,
            out_specs=(pl.BlockSpec(memory_space=pltpu.HBM),) * 2,
            scratch_shapes=[dma((2,))],
            compiler_params=pltpu.CompilerParams(vmem_limit_bytes=1_000_000),
        )(*(result.reshape((1,) + whole) for result in results))

    in_specs = (
        P("batch", None, None),
        P("depth", None, None),
        P("depth", None, None),
        P("depth", None, None),
        P("depth", None, None),
        P("depth", None),
        P("depth", None),
    )
    out_specs = (P("depth", "batch", None, None), P("depth", "batch", None, None))
    return jax.shard_map(
        on_device, mesh=mesh, in_specs=in_specs, out_specs=out_specs, check_vma=False
    )
```

```python
import functools
import math

import jax
import jax.numpy as jnp
from jax import lax
from jax.experimental import pallas as pl
from jax.experimental.pallas import tpu as pltpu
from jax.sharding import PartitionSpec as P

COARSEN = 4
GROUP = 256
PIECES = 2
LAG = 3

step_size = 0.25
epsilon = 1e-06

FIRST, CHAIN, COARSE, RELAX, FINAL = range(5)
STAGES = 5
MESH = pl.DeviceIdType.MESH


def kernel(
    blocks, inputs, h_qkv, h_out, h_up, h_down, h_gain, h_head, states, coarse,
    w_qkv, w_out, w_up, w_down, in_gain, qk_gain, keys_ref, values_ref, load_sem, rx, tx, base, ends, term, share, parts, gathered, same_head, head_scale, query_scale,
    send_sem, recv_sem, share_send, share_recv, ahead_send, own_send, own_recv, back_send,
):
    micro, frames, width = inputs.shape
    head_dim = qk_gain.shape[1]
    rows = frames // COARSEN
    device = lax.axis_index("depth")
    position = lax.rem(device, COARSEN)
    block = device // COARSEN
    has_next = block < blocks - 1
    last = COARSEN - 1
    is_last = position == last

    def columns(ref, part):
        return ref.at[0, :, pl.ds(part * width, width)]

    loads = [
        pltpu.make_async_copy(source, target, load_sem.at[i])
        for i, (source, target) in enumerate((
            (h_head, qk_gain), (h_gain, in_gain), (inputs, rx.at[FIRST]),
            *((columns(h_qkv, part), columns(w_qkv, part)) for part in (1, 0, 2)),
            (h_up, w_up), (h_down, w_down), (h_out, w_out),
        ))
    ]
    load_keys, load_queries, load_values, load_up, load_down, load_out = loads[3:]
    for load in loads:
        load.start()

    def at(depth):
        return {"depth": depth}

    barrier = pltpu.get_barrier_semaphore()
    for i in range(COARSEN):
        @pl.when(block > 0)
        def _():
            pl.semaphore_signal(barrier, inc=1, device_id=at((block - 1) * COARSEN + i), device_id_type=MESH)

        @pl.when(has_next)
        def _():
            pl.semaphore_signal(barrier, inc=1, device_id=at((block + 1) * COARSEN + i), device_id_type=MESH)

    for i in range(1, COARSEN):
        other = block * COARSEN + lax.rem(position + i, COARSEN)
        pl.semaphore_signal(barrier, inc=1, device_id=at(other), device_id_type=MESH)

    heads_of = lax.broadcasted_iota(jnp.int32, (GROUP, GROUP), 0) // head_dim
    heads_at = lax.broadcasted_iota(jnp.int32, (GROUP, GROUP), 1) // head_dim
    same_head[...] = jnp.where(heads_of == heads_at, 1.0, 0.0).astype(jnp.bfloat16)
    keys_ref[...] = jnp.zeros_like(keys_ref)
    values_ref[...] = jnp.zeros_like(values_ref)
    loads[0].wait()
    head_scale[...] = jnp.concatenate([qk_gain[...]] * (width // head_dim), axis=1)
    query_scale[...] = head_scale[...] * (1.0 / math.sqrt(head_dim))

    neighbours = (block > 0).astype(jnp.int32) + has_next.astype(jnp.int32)
    loads[1].wait()
    loads[2].wait()

    def keep(value, load):
        return value

    def fetched(value, load):
        load.wait()
        return value

    def delta(current, unit, after=keep):
        piece = lax.rem(unit, PIECES)
        here = pl.ds(pl.multiple_of(piece * frames, frames), frames)
        spread = jnp.mean(current * current, axis=-1, keepdims=True) + epsilon
        row_scale = lax.rsqrt(spread)
        gained = (current * in_gain[...]).astype(jnp.bfloat16)
        same = same_head[...]
        copies = GROUP // head_dim
        causal = lax.broadcasted_iota(jnp.int32, (frames, GROUP), 0) + piece * frames >= lax.rem(
            lax.broadcasted_iota(jnp.int32, (frames, GROUP), 1), PIECES * frames
        )
        starts = range(0, width, GROUP)
        half = w_up.shape[2] // 2

        def project(part, load):
            return jnp.dot(
                after(gained, load), w_qkv[0, :, part * width:(part + 1) * width], preferred_element_type=jnp.float32
            )

        def head_norm(rows_of, scale_of):
            cut = [rows_of[:, start:start + GROUP] for start in starts]
            squares = jnp.concatenate([(part * part).astype(jnp.bfloat16) for part in cut], axis=0)
            means = jnp.dot(squares, same, preferred_element_type=jnp.float32) * (1.0 / head_dim)
            scales = lax.rsqrt(means + jnp.concatenate([epsilon * spread] * len(cut), axis=0))
            return [
                (part * (scales[i * frames:(i + 1) * frames] * scale_of[:, start:start + GROUP])).astype(jnp.bfloat16)
                for i, (part, start) in enumerate(zip(cut, starts))
            ]

        def raise_half(i):
            raised = jnp.dot(gained, w_up[0, :, i * half:(i + 1) * half], preferred_element_type=jnp.float32)
            return jax.nn.gelu(raised * row_scale, approximate=True).astype(jnp.bfloat16)

        key_rows = project(1, load_keys)
        query_rows = project(0, load_queries)
        keys_of = head_norm(key_rows, head_scale)
        queries_of = head_norm(query_rows, query_scale)
        values_of = (project(2, load_values) * row_scale).astype(jnp.bfloat16)
        after(gained, load_up)
        hidden = raise_half(0)
        weights, mixes = [], []
        for i, start in enumerate(starts):
            part = slice(start, start + GROUP)
            keys_ref[here, part] = keys_of[i]
            values_ref[here, part] = values_of[:, part]
            keys = jnp.concatenate([keys_ref[:, part]] * copies, axis=0) * same
            scores = lax.dot_general(
                queries_of[i], keys, (((1,), (1,)), ((), ())), preferred_element_type=jnp.float32
            )
            weights.append(jnp.where(causal, jnp.exp(scores), 0.0).astype(jnp.bfloat16))
        hidden = jnp.concatenate([hidden, raise_half(1)], axis=1)
        totals = jnp.dot(jnp.concatenate(weights, axis=0), same, preferred_element_type=jnp.float32)
        for weight, start in zip(weights, starts):
            values = jnp.concatenate([values_ref[:, start:start + GROUP]] * copies, axis=0) * same
            mixes.append(jnp.dot(weight, values, preferred_element_type=jnp.float32))
        after(hidden, load_down)
        lowered = jnp.dot(hidden, w_down[0], preferred_element_type=jnp.float32)
        contexts = [
            (mixed / totals[i * frames:(i + 1) * frames]).astype(jnp.bfloat16)
            for i, mixed in enumerate(mixes)
        ]
        context = jnp.concatenate(contexts, axis=1)
        after(context, load_out)
        return jnp.dot(context, w_out[0], preferred_element_type=jnp.float32) + lowered

    def active(stage):
        return (
            ((stage == FIRST) & ((block > 0) | (position == 0)))
            | ((stage == CHAIN) & (position > 0))
            | ((stage == COARSE) & (block > 0))
            | ((stage == RELAX) & (block > 0) & (position > 0))
            | ((stage == FINAL) & (block > 1) & (position < last))
        )

    def passes_on(stage):
        return (
            ((stage == FIRST) & (position == 0))
            | ((stage == CHAIN) & (position > 0) & (position < last))
            | ((stage == COARSE) & (block > 0) & (position == 0))
            | ((stage == RELAX) & (block > 0) & (position > 0) & ((position < last) | has_next))
            | ((stage == FINAL) & (block > 1) & (position < last - 1))
        )

    def is_state(stage):
        return (
            ((stage <= CHAIN) & (block == 0))
            | (((stage == COARSE) | (stage == RELAX)) & (block == 1))
            | ((stage == RELAX) & is_last)
            | (stage == FINAL)
        )

    def hop(stage, seq):
        target = jnp.where(
            stage <= CHAIN, CHAIN, jnp.where((stage == FINAL) | ((stage == RELAX) & is_last), FINAL, RELAX)
        )
        return pltpu.make_async_remote_copy(
            src_ref=tx.at[stage, seq], dst_ref=rx.at[target, seq],
            send_sem=send_sem.at[stage, seq], recv_sem=recv_sem.at[target, seq],
            device_id=at(device + 1), device_id_type=MESH,
        )

    def own_rows(of):
        return pl.ds(pl.multiple_of(of * rows, rows), rows)

    def far_first(i):
        far = last - position
        return (far, lax.rem(position + 2, COARSEN), lax.rem(far + 2, COARSEN), position)[i]

    def give_share(seq, i):
        other = far_first(i - 1)
        return pltpu.make_async_remote_copy(
            src_ref=term.at[seq, own_rows(other)], dst_ref=parts.at[seq, i - 1],
            send_sem=share_send.at[seq, i - 1], recv_sem=share_recv.at[seq],
            device_id=at(block * COARSEN + other), device_id_type=MESH,
        )

    def scatter_end(seq, i):
        return pltpu.make_async_remote_copy(
            src_ref=term.at[seq, own_rows(i)], dst_ref=parts.at[seq, 0],
            send_sem=share_send.at[seq, i], recv_sem=share_recv.at[seq],
            device_id=at(i), device_id_type=MESH,
        )

    def give_ahead(seq, i):
        other = far_first(i)
        return pltpu.make_async_remote_copy(
            src_ref=share.at[seq], dst_ref=rx.at[COARSE, seq, own_rows(position)],
            send_sem=ahead_send.at[seq, i], recv_sem=recv_sem.at[COARSE, seq],
            device_id=at((block + 1) * COARSEN + other), device_id_type=MESH,
        )

    def give_own(seq, i):
        other = far_first(i - 1)
        return pltpu.make_async_remote_copy(
            src_ref=share.at[seq], dst_ref=gathered.at[seq, own_rows(position)],
            send_sem=own_send.at[seq, i - 1], recv_sem=own_recv.at[seq],
            device_id=at(block * COARSEN + other), device_id_type=MESH,
        )

    def landed(ref, sem):
        pltpu.make_async_copy(ref, ref, sem).wait()

    def give_back(seq):
        return pltpu.make_async_remote_copy(
            src_ref=rx.at[COARSE, seq], dst_ref=gathered.at[seq],
            send_sem=back_send.at[seq], recv_sem=own_recv.at[seq],
            device_id=at(device - COARSEN), device_id_type=MESH,
        )

    def finish(seq):
        mine = own_rows(position)

        @pl.when((block == 0) & is_last)
        def _():
            share[seq] = term[seq, mine]

        @pl.when((block == 0) & jnp.logical_not(is_last))
        def _():
            landed(parts.at[seq, 0], share_recv.at[seq])
            share[seq] = parts[seq, 0]

        @pl.when(block > 0)
        def _():
            landed(parts.at[seq], share_recv.at[seq])
            share[seq] = (term[seq, mine] + parts[seq, 0]) + (parts[seq, 1] + parts[seq, 2])

        @pl.when(has_next)
        def _():
            for i in range(COARSEN):
                give_ahead(seq, i).start()

        @pl.when(jnp.logical_not(has_next))
        def _():
            for i in range(1, COARSEN):
                give_own(seq, i).start()
            gathered[seq, mine] = share[seq]

    def turn(step, carry):
        stage, seq = step // micro, lax.rem(step, micro)

        @pl.when(active(stage))
        def _():
            @pl.when(stage > FIRST)
            def _():
                landed(rx.at[stage, seq], recv_sem.at[stage, seq])

            current = rx[stage, seq]
            change = step_size * delta(current, seq)
            moved = current + change

            shares_first = (stage == COARSE) & (block == 1)

            @pl.when(passes_on(stage) & jnp.logical_not(shares_first))
            def _():
                tx[stage, seq] = moved
                hop(stage, seq).start()

            @pl.when(stage == FIRST)
            def _():
                base[seq] = change

            @pl.when((stage == CHAIN) & is_last)
            def _():
                @pl.when(block == 0)
                def _():
                    term[seq] = moved
                    for i in range(last):
                        scatter_end(seq, i).start()
                    finish(seq)

                @pl.when(block > 0)
                def _():
                    ends[seq] = moved - rx[FIRST, seq]

            @pl.when(stage == COARSE)
            def _():
                increment = change - base[seq]

                @pl.when(is_last)
                def _():
                    term[seq] = increment + (ends[seq] + current)

                @pl.when(jnp.logical_not(is_last))
                def _():
                    term[seq] = increment

                for i in range(1, COARSEN):
                    give_share(seq, i).start()

                @pl.when(passes_on(stage) & shares_first)
                def _():
                    tx[stage, seq] = moved
                    hop(stage, seq).start()

                give_back(seq).start()

            @pl.when(is_state(stage))
            def _():
                states[0, seq] = moved

            since = step - COARSE * micro - LAG
            turns = jnp.where((position == 1) & (block > 1), micro, micro - LAG)

            @pl.when((block > 0) & (since >= 0) & (since < turns))
            def _():
                finish(since)

        return carry

    def finish_left(first, last_seq, when):
        for seq in range(first, last_seq):
            @pl.when(when)
            def _():
                finish(seq)

    current = rx[FIRST, 0]
    change = step_size * delta(current, 0, fetched)
    base[0] = change
    pl.semaphore_wait(barrier, COARSEN - 1 + COARSEN * neighbours)
    moved = current + change

    @pl.when(position == 0)
    def _():
        tx[FIRST, 0] = moved
        hop(FIRST, 0).start()

    @pl.when(block == 0)
    def _():
        states[0, 0] = moved

    lax.fori_loop(1, RELAX * micro, turn, 0)
    finish_left(0, micro, (block == 0) & jnp.logical_not(is_last))
    finish_left(max(micro - LAG, 0), micro, (block == 1) | ((block > 1) & (position != 1)))
    lax.fori_loop(RELAX * micro, STAGES * micro, turn, 0)

    for seq in range(micro):
        @pl.when(has_next)
        def _():
            landed(gathered.at[seq], own_recv.at[seq])

        @pl.when(jnp.logical_not(has_next))
        def _():
            landed(gathered.at[seq, pl.ds(0, last * rows)], own_recv.at[seq])

    coarse[0] = gathered[...]

    for seq in range(micro):
        for stage in range(STAGES):
            @pl.when(passes_on(stage))
            def _():
                hop(stage, seq).wait_send()

        @pl.when((block == 0) & is_last)
        def _():
            for i in range(last):
                scatter_end(seq, i).wait_send()

        @pl.when(block > 0)
        def _():
            for i in range(1, COARSEN):
                give_share(seq, i).wait_send()
            give_back(seq).wait_send()

        @pl.when(has_next)
        def _():
            for i in range(COARSEN):
                give_ahead(seq, i).wait_send()

        @pl.when(jnp.logical_not(has_next))
        def _():
            for i in range(1, COARSEN):
                give_own(seq, i).wait_send()


def hand_over(states, coarse, states_out, coarse_out, sem):
    copies = [
        pltpu.make_async_copy(source, target, sem.at[i])
        for i, (source, target) in enumerate(((states, states_out), (coarse, coarse_out)))
    ]
    for copy in copies:
        copy.start()
    for copy in copies:
        copy.wait()


def solution(mesh):
    blocks = mesh.shape["depth"] // COARSEN

    def on_device(inputs, attn_in, attn_out, mlp_in, mlp_out, norm_gain, head_gain):
        whole = inputs.shape
        micro, frames, width = whole[0] * PIECES, whole[1] // PIECES, whole[2]
        rows = frames // COARSEN
        state = (micro, frames, width)
        out = jax.ShapeDtypeStruct((1,) + state, jnp.float32)
        vmem = pl.BlockSpec(memory_space=pltpu.VMEM)
        dma = pltpu.SemaphoreType.DMA
        weights = (attn_in, attn_out, mlp_in, mlp_out, norm_gain, head_gain)
        results = pl.pallas_call(
            functools.partial(kernel, blocks),
            out_shape=(out, out),
            in_specs=[pl.BlockSpec(memory_space=pl.ANY)] * 7,
            out_specs=(vmem, vmem),
            scratch_shapes=[
                *(pltpu.VMEM(weight.shape, weight.dtype) for weight in weights),
                pltpu.VMEM(whole[1:], jnp.bfloat16),
                pltpu.VMEM(whole[1:], jnp.bfloat16),
                dma((len(weights) + 3,)),
                pltpu.VMEM((STAGES,) + state, jnp.float32),
                pltpu.VMEM((STAGES,) + state, jnp.float32),
                pltpu.VMEM(state, jnp.float32),
                pltpu.VMEM(state, jnp.float32),
                pltpu.VMEM(state, jnp.float32),
                pltpu.VMEM((micro, rows, width), jnp.float32),
                pltpu.VMEM((micro, COARSEN - 1, rows, width), jnp.float32),
                pltpu.VMEM(state, jnp.float32),
                pltpu.VMEM((GROUP, GROUP), jnp.bfloat16),
                pltpu.VMEM((1, width), jnp.float32),
                pltpu.VMEM((1, width), jnp.float32),
                dma((STAGES, micro)),
                dma((STAGES, micro)),
                dma((micro, COARSEN - 1)),
                dma((micro,)),
                dma((micro, COARSEN)),
                dma((micro, COARSEN - 1)),
                dma((micro,)),
                dma((micro,)),
            ],
            compiler_params=pltpu.CompilerParams(
                collective_id=0, has_side_effects=True, vmem_limit_bytes=56_000_000,
            ),
        )(*(pltpu.with_memory_space_constraint(v, pltpu.HBM) for v in (inputs.reshape(state), *weights)))
        return pl.pallas_call(
            hand_over,
            out_shape=(jax.ShapeDtypeStruct((1,) + whole, jnp.float32),) * 2,
            in_specs=[pl.BlockSpec(memory_space=pl.ANY)] * 2,
            out_specs=(pl.BlockSpec(memory_space=pltpu.HBM),) * 2,
            scratch_shapes=[dma((2,))],
            compiler_params=pltpu.CompilerParams(vmem_limit_bytes=1_000_000),
        )(*(result.reshape((1,) + whole) for result in results))

    in_specs = (
        P("batch", None, None),
        P("depth", None, None),
        P("depth", None, None),
        P("depth", None, None),
        P("depth", None, None),
        P("depth", None),
        P("depth", None),
    )
    out_specs = (P("depth", "batch", None, None), P("depth", "batch", None, None))
    return jax.shard_map(
        on_device, mesh=mesh, in_specs=in_specs, out_specs=out_specs, check_vma=False
    )
```

```python
import functools
import math

import jax
import jax.numpy as jnp
from jax import lax
from jax.experimental import pallas as pl
from jax.experimental.pallas import tpu as pltpu
from jax.sharding import PartitionSpec as P

COARSEN = 4
GROUP = 256
PIECES = 2
LAG = 4

step_size = 0.25
epsilon = 1e-06

FIRST, CHAIN, COARSE, RELAX, FINAL = range(5)
STAGES = 5
MESH = pl.DeviceIdType.MESH


def kernel(
    blocks, inputs, h_qkv, h_out, h_up, h_down, h_gain, h_head, states, coarse,
    w_qkv, w_out, w_up, w_down, in_gain, qk_gain, keys_ref, values_ref, load_sem, rx, tx, base, ends, term, share, parts, gathered, same_head, head_scale, query_scale,
    send_sem, recv_sem, share_send, share_recv, ahead_send, own_send, own_recv, back_send,
):
    micro, frames, width = inputs.shape
    head_dim = qk_gain.shape[1]
    rows = frames // COARSEN
    device = lax.axis_index("depth")
    position = lax.rem(device, COARSEN)
    block = device // COARSEN
    has_next = block < blocks - 1
    last = COARSEN - 1
    is_last = position == last

    def columns(ref, part):
        return ref.at[0, :, pl.ds(part * width, width)]

    loads = [
        pltpu.make_async_copy(source, target, load_sem.at[i])
        for i, (source, target) in enumerate((
            (h_head, qk_gain), (h_gain, in_gain), (inputs, rx.at[FIRST]),
            *((columns(h_qkv, part), columns(w_qkv, part)) for part in (1, 0, 2)),
            (h_up, w_up), (h_down, w_down), (h_out, w_out),
        ))
    ]
    load_keys, load_queries, load_values, load_up, load_down, load_out = loads[3:]
    for load in loads:
        load.start()

    def at(depth):
        return {"depth": depth}

    barrier = pltpu.get_barrier_semaphore()
    for i in range(COARSEN):
        @pl.when(block > 0)
        def _():
            pl.semaphore_signal(barrier, inc=1, device_id=at((block - 1) * COARSEN + i), device_id_type=MESH)

        @pl.when(has_next)
        def _():
            pl.semaphore_signal(barrier, inc=1, device_id=at((block + 1) * COARSEN + i), device_id_type=MESH)

    for i in range(1, COARSEN):
        other = block * COARSEN + lax.rem(position + i, COARSEN)
        pl.semaphore_signal(barrier, inc=1, device_id=at(other), device_id_type=MESH)

    heads_of = lax.broadcasted_iota(jnp.int32, (GROUP, GROUP), 0) // head_dim
    heads_at = lax.broadcasted_iota(jnp.int32, (GROUP, GROUP), 1) // head_dim
    same_head[...] = jnp.where(heads_of == heads_at, 1.0, 0.0).astype(jnp.bfloat16)
    keys_ref[...] = jnp.zeros_like(keys_ref)
    values_ref[...] = jnp.zeros_like(values_ref)
    loads[0].wait()
    head_scale[...] = jnp.concatenate([qk_gain[...]] * (width // head_dim), axis=1)
    query_scale[...] = head_scale[...] * (math.log2(math.e) / math.sqrt(head_dim))

    neighbours = (block > 0).astype(jnp.int32) + has_next.astype(jnp.int32)
    loads[1].wait()
    loads[2].wait()

    def keep(value, load):
        return value

    def fetched(value, load):
        load.wait()
        return value

    def delta(current, unit, after=keep):
        piece = lax.rem(unit, PIECES)
        here = pl.ds(pl.multiple_of(piece * frames, frames), frames)
        spread = jnp.mean(current * current, axis=-1, keepdims=True) + epsilon
        row_scale = lax.rsqrt(spread)
        gained = (current * in_gain[...]).astype(jnp.bfloat16)
        same = same_head[...]
        copies = GROUP // head_dim
        causal = lax.broadcasted_iota(jnp.int32, (frames, GROUP), 0) + piece * frames >= lax.rem(
            lax.broadcasted_iota(jnp.int32, (frames, GROUP), 1), PIECES * frames
        )
        starts = range(0, width, GROUP)
        half = w_up.shape[2] // 2

        def project(part, load):
            return jnp.dot(
                after(gained, load), w_qkv[0, :, part * width:(part + 1) * width], preferred_element_type=jnp.float32
            )

        def head_norm(rows_of, scale_of):
            cut = [rows_of[:, start:start + GROUP] for start in starts]
            squares = jnp.concatenate([(part * part).astype(jnp.bfloat16) for part in cut], axis=0)
            means = jnp.dot(squares, same, preferred_element_type=jnp.float32) * (1.0 / head_dim)
            scales = lax.rsqrt(means + jnp.concatenate([epsilon * spread] * len(cut), axis=0))
            return [
                (part * (scales[i * frames:(i + 1) * frames] * scale_of[:, start:start + GROUP])).astype(jnp.bfloat16)
                for i, (part, start) in enumerate(zip(cut, starts))
            ]

        def raise_half(i):
            raised = jnp.dot(gained, w_up[0, :, i * half:(i + 1) * half], preferred_element_type=jnp.float32)
            return jax.nn.gelu(raised * row_scale, approximate=True).astype(jnp.bfloat16)

        key_rows = project(1, load_keys)
        query_rows = project(0, load_queries)
        keys_of = head_norm(key_rows, head_scale)
        queries_of = head_norm(query_rows, query_scale)
        values_of = (project(2, load_values) * row_scale).astype(jnp.bfloat16)
        after(gained, load_up)
        hidden = raise_half(0)
        weights, mixes = [], []
        for i, start in enumerate(starts):
            part = slice(start, start + GROUP)
            keys_ref[here, part] = keys_of[i]
            values_ref[here, part] = values_of[:, part]
            keys = jnp.concatenate([keys_ref[:, part]] * copies, axis=0) * same
            scores = lax.dot_general(
                queries_of[i], keys, (((1,), (1,)), ((), ())), preferred_element_type=jnp.float32
            )
            weights.append(jnp.where(causal, jnp.exp2(scores), 0.0).astype(jnp.bfloat16))
        hidden = jnp.concatenate([hidden, raise_half(1)], axis=1)
        totals = jnp.dot(jnp.concatenate(weights, axis=0), same, preferred_element_type=jnp.float32)
        for weight, start in zip(weights, starts):
            values = jnp.concatenate([values_ref[:, start:start + GROUP]] * copies, axis=0) * same
            mixes.append(jnp.dot(weight, values, preferred_element_type=jnp.float32))
        after(hidden, load_down)
        lowered = jnp.dot(hidden, w_down[0], preferred_element_type=jnp.float32)
        contexts = [
            (mixed / totals[i * frames:(i + 1) * frames]).astype(jnp.bfloat16)
            for i, mixed in enumerate(mixes)
        ]
        context = jnp.concatenate(contexts, axis=1)
        after(context, load_out)
        return jnp.dot(context, w_out[0], preferred_element_type=jnp.float32) + lowered

    def active(stage):
        return (
            ((stage == FIRST) & ((block > 0) | (position == 0)))
            | ((stage == CHAIN) & (position > 0))
            | ((stage == COARSE) & (block > 0))
            | ((stage == RELAX) & (block > 0) & (position > 0))
            | ((stage == FINAL) & (block > 1) & (position < last))
        )

    def passes_on(stage):
        return (
            ((stage == FIRST) & (position == 0))
            | ((stage == CHAIN) & (position > 0) & (position < last))
            | ((stage == COARSE) & (block > 0) & (position == 0))
            | ((stage == RELAX) & (block > 0) & (position > 0) & ((position < last) | has_next))
            | ((stage == FINAL) & (block > 1) & (position < last - 1))
        )

    def is_state(stage):
        return (
            ((stage <= CHAIN) & (block == 0))
            | (((stage == COARSE) | (stage == RELAX)) & (block == 1))
            | ((stage == RELAX) & is_last)
            | (stage == FINAL)
        )

    def hop(stage, seq):
        target = jnp.where(
            stage <= CHAIN, CHAIN, jnp.where((stage == FINAL) | ((stage == RELAX) & is_last), FINAL, RELAX)
        )
        return pltpu.make_async_remote_copy(
            src_ref=tx.at[stage, seq], dst_ref=rx.at[target, seq],
            send_sem=send_sem.at[stage, seq], recv_sem=recv_sem.at[target, seq],
            device_id=at(device + 1), device_id_type=MESH,
        )

    def own_rows(of):
        return pl.ds(pl.multiple_of(of * rows, rows), rows)

    def far_first(i):
        far = last - position
        return (far, lax.rem(position + 2, COARSEN), lax.rem(far + 2, COARSEN), position)[i]

    def give_share(seq, i):
        other = far_first(i - 1)
        return pltpu.make_async_remote_copy(
            src_ref=term.at[seq, own_rows(other)], dst_ref=parts.at[seq, i - 1],
            send_sem=share_send.at[seq, i - 1], recv_sem=share_recv.at[seq],
            device_id=at(block * COARSEN + other), device_id_type=MESH,
        )

    def scatter_end(seq, i):
        return pltpu.make_async_remote_copy(
            src_ref=term.at[seq, own_rows(i)], dst_ref=parts.at[seq, 0],
            send_sem=share_send.at[seq, i], recv_sem=share_recv.at[seq],
            device_id=at(i), device_id_type=MESH,
        )

    def give_ahead(seq, i):
        other = far_first(i)
        return pltpu.make_async_remote_copy(
            src_ref=share.at[seq], dst_ref=rx.at[COARSE, seq, own_rows(position)],
            send_sem=ahead_send.at[seq, i], recv_sem=recv_sem.at[COARSE, seq],
            device_id=at((block + 1) * COARSEN + other), device_id_type=MESH,
        )

    def give_own(seq, i):
        other = far_first(i - 1)
        return pltpu.make_async_remote_copy(
            src_ref=share.at[seq], dst_ref=gathered.at[seq, own_rows(position)],
            send_sem=own_send.at[seq, i - 1], recv_sem=own_recv.at[seq],
            device_id=at(block * COARSEN + other), device_id_type=MESH,
        )

    def landed(ref, sem):
        pltpu.make_async_copy(ref, ref, sem).wait()

    def give_back(seq):
        return pltpu.make_async_remote_copy(
            src_ref=rx.at[COARSE, seq], dst_ref=gathered.at[seq],
            send_sem=back_send.at[seq], recv_sem=own_recv.at[seq],
            device_id=at(device - COARSEN), device_id_type=MESH,
        )

    def finish(seq):
        mine = own_rows(position)

        @pl.when((block == 0) & is_last)
        def _():
            share[seq] = term[seq, mine]

        @pl.when((block == 0) & jnp.logical_not(is_last))
        def _():
            landed(parts.at[seq, 0], share_recv.at[seq])
            share[seq] = parts[seq, 0]

        @pl.when(block > 0)
        def _():
            landed(parts.at[seq], share_recv.at[seq])
            share[seq] = (term[seq, mine] + parts[seq, 0]) + (parts[seq, 1] + parts[seq, 2])

        @pl.when(has_next)
        def _():
            for i in range(COARSEN):
                give_ahead(seq, i).start()

        @pl.when(jnp.logical_not(has_next))
        def _():
            for i in range(1, COARSEN):
                give_own(seq, i).start()
            gathered[seq, mine] = share[seq]

    def turn(step, carry):
        stage, seq = step // micro, lax.rem(step, micro)

        @pl.when(active(stage))
        def _():
            @pl.when(stage > FIRST)
            def _():
                landed(rx.at[stage, seq], recv_sem.at[stage, seq])

            current = rx[stage, seq]
            change = step_size * delta(current, seq)
            moved = current + change

            shares_first = (stage == COARSE) & (block == 1)

            @pl.when(passes_on(stage) & jnp.logical_not(shares_first))
            def _():
                tx[stage, seq] = moved
                hop(stage, seq).start()

            @pl.when(stage == FIRST)
            def _():
                base[seq] = change

            @pl.when((stage == CHAIN) & is_last)
            def _():
                @pl.when(block == 0)
                def _():
                    term[seq] = moved
                    for i in range(last):
                        scatter_end(seq, i).start()
                    finish(seq)

                @pl.when(block > 0)
                def _():
                    ends[seq] = moved - rx[FIRST, seq]

            @pl.when(stage == COARSE)
            def _():
                increment = change - base[seq]

                @pl.when(is_last)
                def _():
                    term[seq] = increment + (ends[seq] + current)

                @pl.when(jnp.logical_not(is_last))
                def _():
                    term[seq] = increment

                for i in range(1, COARSEN):
                    give_share(seq, i).start()

                @pl.when(passes_on(stage) & shares_first)
                def _():
                    tx[stage, seq] = moved
                    hop(stage, seq).start()

                give_back(seq).start()

            @pl.when(is_state(stage))
            def _():
                states[0, seq] = moved

            since = step - COARSE * micro - LAG
            turns = jnp.where((position == 1) & (block > 1), micro, micro - LAG)

            @pl.when((block > 0) & (since >= 0) & (since < turns))
            def _():
                finish(since)

        return carry

    def finish_left(first, last_seq, when):
        for seq in range(first, last_seq):
            @pl.when(when)
            def _():
                finish(seq)

    current = rx[FIRST, 0]
    change = step_size * delta(current, 0, fetched)
    base[0] = change
    pl.semaphore_wait(barrier, COARSEN - 1 + COARSEN * neighbours)
    moved = current + change

    @pl.when(position == 0)
    def _():
        tx[FIRST, 0] = moved
        hop(FIRST, 0).start()

    @pl.when(block == 0)
    def _():
        states[0, 0] = moved

    lax.fori_loop(1, RELAX * micro, turn, 0)
    finish_left(0, micro, (block == 0) & jnp.logical_not(is_last))
    finish_left(max(micro - LAG, 0), micro, (block == 1) | ((block > 1) & (position != 1)))
    lax.fori_loop(RELAX * micro, STAGES * micro, turn, 0)

    for seq in range(micro):
        @pl.when(has_next)
        def _():
            landed(gathered.at[seq], own_recv.at[seq])

        @pl.when(jnp.logical_not(has_next))
        def _():
            landed(gathered.at[seq, pl.ds(0, last * rows)], own_recv.at[seq])

    coarse[0] = gathered[...]

    for seq in range(micro):
        for stage in range(STAGES):
            @pl.when(passes_on(stage))
            def _():
                hop(stage, seq).wait_send()

        @pl.when((block == 0) & is_last)
        def _():
            for i in range(last):
                scatter_end(seq, i).wait_send()

        @pl.when(block > 0)
        def _():
            for i in range(1, COARSEN):
                give_share(seq, i).wait_send()
            give_back(seq).wait_send()

        @pl.when(has_next)
        def _():
            for i in range(COARSEN):
                give_ahead(seq, i).wait_send()

        @pl.when(jnp.logical_not(has_next))
        def _():
            for i in range(1, COARSEN):
                give_own(seq, i).wait_send()


def hand_over(states, coarse, states_out, coarse_out, sem):
    copies = [
        pltpu.make_async_copy(source, target, sem.at[i])
        for i, (source, target) in enumerate(
            (source.at[0, part], target.at[0, part])
            for source, target in ((states, states_out), (coarse, coarse_out))
            for part in range(states.shape[1])
        )
    ]
    for copy in copies:
        copy.start()
    for copy in copies:
        copy.wait()


def solution(mesh):
    blocks = mesh.shape["depth"] // COARSEN

    def on_device(inputs, attn_in, attn_out, mlp_in, mlp_out, norm_gain, head_gain):
        whole = inputs.shape
        micro, frames, width = whole[0] * PIECES, whole[1] // PIECES, whole[2]
        rows = frames // COARSEN
        state = (micro, frames, width)
        out = jax.ShapeDtypeStruct((1,) + state, jnp.float32)
        vmem = pl.BlockSpec(memory_space=pltpu.VMEM)
        dma = pltpu.SemaphoreType.DMA
        weights = (attn_in, attn_out, mlp_in, mlp_out, norm_gain, head_gain)
        results = pl.pallas_call(
            functools.partial(kernel, blocks),
            out_shape=(out, out),
            in_specs=[pl.BlockSpec(memory_space=pl.ANY)] * 7,
            out_specs=(vmem, vmem),
            scratch_shapes=[
                *(pltpu.VMEM(weight.shape, weight.dtype) for weight in weights),
                pltpu.VMEM(whole[1:], jnp.bfloat16),
                pltpu.VMEM(whole[1:], jnp.bfloat16),
                dma((len(weights) + 3,)),
                pltpu.VMEM((STAGES,) + state, jnp.float32),
                pltpu.VMEM((STAGES,) + state, jnp.float32),
                pltpu.VMEM(state, jnp.float32),
                pltpu.VMEM(state, jnp.float32),
                pltpu.VMEM(state, jnp.float32),
                pltpu.VMEM((micro, rows, width), jnp.float32),
                pltpu.VMEM((micro, COARSEN - 1, rows, width), jnp.float32),
                pltpu.VMEM(state, jnp.float32),
                pltpu.VMEM((GROUP, GROUP), jnp.bfloat16),
                pltpu.VMEM((1, width), jnp.float32),
                pltpu.VMEM((1, width), jnp.float32),
                dma((STAGES, micro)),
                dma((STAGES, micro)),
                dma((micro, COARSEN - 1)),
                dma((micro,)),
                dma((micro, COARSEN)),
                dma((micro, COARSEN - 1)),
                dma((micro,)),
                dma((micro,)),
            ],
            compiler_params=pltpu.CompilerParams(
                collective_id=0, has_side_effects=True, vmem_limit_bytes=56_000_000,
            ),
        )(*(pltpu.with_memory_space_constraint(v, pltpu.HBM) for v in (inputs.reshape(state), *weights)))
        return pl.pallas_call(
            hand_over,
            out_shape=(jax.ShapeDtypeStruct((1,) + whole, jnp.float32),) * 2,
            in_specs=[pl.BlockSpec(memory_space=pl.ANY)] * 2,
            out_specs=(pl.BlockSpec(memory_space=pltpu.HBM),) * 2,
            scratch_shapes=[dma((2 * whole[0],))],
            compiler_params=pltpu.CompilerParams(vmem_limit_bytes=1_000_000),
        )(*(result.reshape((1,) + whole) for result in results))

    in_specs = (
        P("batch", None, None),
        P("depth", None, None),
        P("depth", None, None),
        P("depth", None, None),
        P("depth", None, None),
        P("depth", None),
        P("depth", None),
    )
    out_specs = (P("depth", "batch", None, None), P("depth", "batch", None, None))
    return jax.shard_map(
        on_device, mesh=mesh, in_specs=in_specs, out_specs=out_specs, check_vma=False
    )
```

```python
import functools
import math

import jax
import jax.numpy as jnp
from jax import lax
from jax.experimental import pallas as pl
from jax.experimental.pallas import tpu as pltpu
from jax.sharding import PartitionSpec as P

COARSEN = 4
GROUP = 256
PIECES = 2
LAG = 4

step_size = 0.25
epsilon = 1e-06

FIRST, CHAIN, COARSE, RELAX, FINAL = range(5)
STAGES = 5
MESH = pl.DeviceIdType.MESH


def kernel(
    blocks, inputs, h_qkv, h_out, h_up, h_down, h_gain, h_head, states, coarse,
    w_qkv, w_out, w_up, w_down, in_gain, qk_gain, keys_ref, values_ref, load_sem, rx, tx, base, ends, term, share, parts, gathered, same_head, head_scale, query_scale,
    send_sem, recv_sem, share_send, share_recv, ahead_send, own_send, own_recv, back_send,
):
    micro, frames, width = inputs.shape
    head_dim = qk_gain.shape[1]
    rows = frames // COARSEN
    device = lax.axis_index("depth")
    position = lax.rem(device, COARSEN)
    block = device // COARSEN
    has_next = block < blocks - 1
    last = COARSEN - 1
    is_last = position == last

    def columns(ref, part):
        return ref.at[0, :, pl.ds(part * width, width)]

    loads = [
        pltpu.make_async_copy(source, target, load_sem.at[i])
        for i, (source, target) in enumerate((
            (h_head, qk_gain), (h_gain, in_gain), (inputs, rx.at[FIRST]),
            *((columns(h_qkv, part), columns(w_qkv, part)) for part in (1, 0, 2)),
            (h_up, w_up), (h_down, w_down), (h_out, w_out),
        ))
    ]
    load_keys, load_queries, load_values, load_up, load_down, load_out = loads[3:]
    for load in loads:
        load.start()

    def at(depth):
        return {"depth": depth}

    barrier = pltpu.get_barrier_semaphore()
    for i in range(COARSEN):
        @pl.when(block > 0)
        def _():
            pl.semaphore_signal(barrier, inc=1, device_id=at((block - 1) * COARSEN + i), device_id_type=MESH)

        @pl.when(has_next)
        def _():
            pl.semaphore_signal(barrier, inc=1, device_id=at((block + 1) * COARSEN + i), device_id_type=MESH)

    for i in range(1, COARSEN):
        other = block * COARSEN + lax.rem(position + i, COARSEN)
        pl.semaphore_signal(barrier, inc=1, device_id=at(other), device_id_type=MESH)

    heads_of = lax.broadcasted_iota(jnp.int32, (GROUP, GROUP), 0) // head_dim
    heads_at = lax.broadcasted_iota(jnp.int32, (GROUP, GROUP), 1) // head_dim
    same_head[...] = jnp.where(heads_of == heads_at, 1.0, 0.0).astype(jnp.bfloat16)
    keys_ref[...] = jnp.zeros_like(keys_ref)
    values_ref[...] = jnp.zeros_like(values_ref)
    loads[0].wait()
    head_scale[...] = jnp.concatenate([qk_gain[...]] * (width // head_dim), axis=1)
    query_scale[...] = head_scale[...] * (math.log2(math.e) / math.sqrt(head_dim))

    neighbours = (block > 0).astype(jnp.int32) + has_next.astype(jnp.int32)
    loads[1].wait()
    loads[2].wait()

    def keep(value, load):
        return value

    def fetched(value, load):
        load.wait()
        return value

    def delta(current, unit, after=keep):
        piece = lax.rem(unit, PIECES)
        here = pl.ds(pl.multiple_of(piece * frames, frames), frames)
        spread = jnp.mean(current * current, axis=-1, keepdims=True) + epsilon
        row_scale = lax.rsqrt(spread)
        gained = (current * in_gain[...]).astype(jnp.bfloat16)
        same = same_head[...]
        copies = GROUP // head_dim
        causal = lax.broadcasted_iota(jnp.int32, (frames, GROUP), 0) + piece * frames >= lax.rem(
            lax.broadcasted_iota(jnp.int32, (frames, GROUP), 1), PIECES * frames
        )
        starts = range(0, width, GROUP)
        half = w_up.shape[2] // 2

        def project(part, load):
            return jnp.dot(
                after(gained, load), w_qkv[0, :, part * width:(part + 1) * width], preferred_element_type=jnp.float32
            )

        def head_norm(rows_of, scale_of):
            cut = [rows_of[:, start:start + GROUP] for start in starts]
            squares = jnp.concatenate([(part * part).astype(jnp.bfloat16) for part in cut], axis=0)
            means = jnp.dot(squares, same, preferred_element_type=jnp.float32) * (1.0 / head_dim)
            scales = lax.rsqrt(means + jnp.concatenate([epsilon * spread] * len(cut), axis=0))
            return [
                (part * (scales[i * frames:(i + 1) * frames] * scale_of[:, start:start + GROUP])).astype(jnp.bfloat16)
                for i, (part, start) in enumerate(zip(cut, starts))
            ]

        def raise_half(i):
            raised = jnp.dot(gained, w_up[0, :, i * half:(i + 1) * half], preferred_element_type=jnp.float32)
            return jax.nn.gelu(raised * row_scale, approximate=True).astype(jnp.bfloat16)

        key_rows = project(1, load_keys)
        query_rows = project(0, load_queries)
        keys_of = head_norm(key_rows, head_scale)
        queries_of = head_norm(query_rows, query_scale)
        values_of = (project(2, load_values) * row_scale).astype(jnp.bfloat16)
        after(gained, load_up)
        hidden = raise_half(0)
        weights, mixes = [], []
        for i, start in enumerate(starts):
            part = slice(start, start + GROUP)
            keys_ref[here, part] = keys_of[i]
            values_ref[here, part] = values_of[:, part]
            keys = jnp.concatenate([keys_ref[:, part]] * copies, axis=0) * same
            scores = lax.dot_general(
                queries_of[i], keys, (((1,), (1,)), ((), ())), preferred_element_type=jnp.float32
            )
            weights.append(jnp.exp2(jnp.where(causal, scores, -jnp.inf)).astype(jnp.bfloat16))
        hidden = jnp.concatenate([hidden, raise_half(1)], axis=1)
        totals = jnp.dot(jnp.concatenate(weights, axis=0), same, preferred_element_type=jnp.float32)
        for weight, start in zip(weights, starts):
            values = jnp.concatenate([values_ref[:, start:start + GROUP]] * copies, axis=0) * same
            mixes.append(jnp.dot(weight, values, preferred_element_type=jnp.float32))
        after(hidden, load_down)
        lowered = jnp.dot(hidden, w_down[0], preferred_element_type=jnp.float32)
        contexts = [
            (mixed / totals[i * frames:(i + 1) * frames]).astype(jnp.bfloat16)
            for i, mixed in enumerate(mixes)
        ]
        context = jnp.concatenate(contexts, axis=1)
        after(context, load_out)
        return jnp.dot(context, w_out[0], preferred_element_type=jnp.float32) + lowered

    def active(stage):
        return (
            ((stage == FIRST) & ((block > 0) | (position == 0)))
            | ((stage == CHAIN) & (position > 0))
            | ((stage == COARSE) & (block > 0))
            | ((stage == RELAX) & (block > 0) & (position > 0))
            | ((stage == FINAL) & (block > 1) & (position < last))
        )

    def passes_on(stage):
        return (
            ((stage == FIRST) & (position == 0))
            | ((stage == CHAIN) & (position > 0) & (position < last))
            | ((stage == COARSE) & (block > 0) & (position == 0))
            | ((stage == RELAX) & (block > 0) & (position > 0) & ((position < last) | has_next))
            | ((stage == FINAL) & (block > 1) & (position < last - 1))
        )

    def is_state(stage):
        return (
            ((stage <= CHAIN) & (block == 0))
            | (((stage == COARSE) | (stage == RELAX)) & (block == 1))
            | ((stage == RELAX) & is_last)
            | (stage == FINAL)
        )

    def hop(stage, seq):
        target = jnp.where(
            stage <= CHAIN, CHAIN, jnp.where((stage == FINAL) | ((stage == RELAX) & is_last), FINAL, RELAX)
        )
        return pltpu.make_async_remote_copy(
            src_ref=tx.at[stage, seq], dst_ref=rx.at[target, seq],
            send_sem=send_sem.at[stage, seq], recv_sem=recv_sem.at[target, seq],
            device_id=at(device + 1), device_id_type=MESH,
        )

    def own_rows(of):
        return pl.ds(pl.multiple_of(of * rows, rows), rows)

    def far_first(i):
        far = last - position
        return (far, lax.rem(position + 2, COARSEN), lax.rem(far + 2, COARSEN), position)[i]

    def give_share(seq, i):
        other = far_first(i - 1)
        return pltpu.make_async_remote_copy(
            src_ref=term.at[seq, own_rows(other)], dst_ref=parts.at[seq, i - 1],
            send_sem=share_send.at[seq, i - 1], recv_sem=share_recv.at[seq],
            device_id=at(block * COARSEN + other), device_id_type=MESH,
        )

    def scatter_end(seq, i):
        return pltpu.make_async_remote_copy(
            src_ref=term.at[seq, own_rows(i)], dst_ref=parts.at[seq, 0],
            send_sem=share_send.at[seq, i], recv_sem=share_recv.at[seq],
            device_id=at(i), device_id_type=MESH,
        )

    def give_ahead(seq, i):
        other = far_first(i)
        return pltpu.make_async_remote_copy(
            src_ref=share.at[seq], dst_ref=rx.at[COARSE, seq, own_rows(position)],
            send_sem=ahead_send.at[seq, i], recv_sem=recv_sem.at[COARSE, seq],
            device_id=at((block + 1) * COARSEN + other), device_id_type=MESH,
        )

    def give_own(seq, i):
        other = far_first(i - 1)
        return pltpu.make_async_remote_copy(
            src_ref=share.at[seq], dst_ref=gathered.at[seq, own_rows(position)],
            send_sem=own_send.at[seq, i - 1], recv_sem=own_recv.at[seq],
            device_id=at(block * COARSEN + other), device_id_type=MESH,
        )

    def landed(ref, sem):
        pltpu.make_async_copy(ref, ref, sem).wait()

    def give_back(seq):
        return pltpu.make_async_remote_copy(
            src_ref=rx.at[COARSE, seq], dst_ref=gathered.at[seq],
            send_sem=back_send.at[seq], recv_sem=own_recv.at[seq],
            device_id=at(device - COARSEN), device_id_type=MESH,
        )

    def finish(seq):
        mine = own_rows(position)

        @pl.when((block == 0) & is_last)
        def _():
            share[seq] = term[seq, mine]

        @pl.when((block == 0) & jnp.logical_not(is_last))
        def _():
            landed(parts.at[seq, 0], share_recv.at[seq])
            share[seq] = parts[seq, 0]

        @pl.when(block > 0)
        def _():
            landed(parts.at[seq], share_recv.at[seq])
            share[seq] = (term[seq, mine] + parts[seq, 0]) + (parts[seq, 1] + parts[seq, 2])

        @pl.when(has_next)
        def _():
            for i in range(COARSEN):
                give_ahead(seq, i).start()

        @pl.when(jnp.logical_not(has_next))
        def _():
            for i in range(1, COARSEN):
                give_own(seq, i).start()
            gathered[seq, mine] = share[seq]

    def turn(step, carry):
        stage, seq = step // micro, lax.rem(step, micro)

        @pl.when(active(stage))
        def _():
            @pl.when(stage > FIRST)
            def _():
                landed(rx.at[stage, seq], recv_sem.at[stage, seq])

            current = rx[stage, seq]
            change = step_size * delta(current, seq)
            moved = current + change

            shares_first = (stage == COARSE) & (block == 1)

            @pl.when(passes_on(stage) & jnp.logical_not(shares_first))
            def _():
                tx[stage, seq] = moved
                hop(stage, seq).start()

            @pl.when(stage == FIRST)
            def _():
                base[seq] = change

            @pl.when((stage == CHAIN) & is_last)
            def _():
                @pl.when(block == 0)
                def _():
                    term[seq] = moved
                    for i in range(last):
                        scatter_end(seq, i).start()
                    finish(seq)

                @pl.when(block > 0)
                def _():
                    ends[seq] = moved - rx[FIRST, seq]

            @pl.when(stage == COARSE)
            def _():
                increment = change - base[seq]

                @pl.when(is_last)
                def _():
                    term[seq] = increment + (ends[seq] + current)

                @pl.when(jnp.logical_not(is_last))
                def _():
                    term[seq] = increment

                for i in range(1, COARSEN):
                    give_share(seq, i).start()

                @pl.when(passes_on(stage) & shares_first)
                def _():
                    tx[stage, seq] = moved
                    hop(stage, seq).start()

                give_back(seq).start()

            @pl.when(is_state(stage))
            def _():
                states[0, seq] = moved

            since = step - COARSE * micro - LAG
            turns = jnp.where((position == 1) & (block > 1), micro, micro - LAG)

            @pl.when((block > 0) & (since >= 0) & (since < turns))
            def _():
                finish(since)

        return carry

    def finish_left(first, last_seq, when):
        for seq in range(first, last_seq):
            @pl.when(when)
            def _():
                finish(seq)

    current = rx[FIRST, 0]
    change = step_size * delta(current, 0, fetched)
    base[0] = change
    pl.semaphore_wait(barrier, COARSEN - 1 + COARSEN * neighbours)
    moved = current + change

    @pl.when(position == 0)
    def _():
        tx[FIRST, 0] = moved
        hop(FIRST, 0).start()

    @pl.when(block == 0)
    def _():
        states[0, 0] = moved

    lax.fori_loop(1, RELAX * micro, turn, 0)
    finish_left(0, micro, (block == 0) & jnp.logical_not(is_last))
    finish_left(max(micro - LAG, 0), micro, (block == 1) | ((block > 1) & (position != 1)))
    lax.fori_loop(RELAX * micro, STAGES * micro, turn, 0)

    for seq in range(micro):
        @pl.when(has_next)
        def _():
            landed(gathered.at[seq], own_recv.at[seq])

        @pl.when(jnp.logical_not(has_next))
        def _():
            landed(gathered.at[seq, pl.ds(0, last * rows)], own_recv.at[seq])

    coarse[0] = gathered[...]

    for seq in range(micro):
        for stage in range(STAGES):
            @pl.when(passes_on(stage))
            def _():
                hop(stage, seq).wait_send()

        @pl.when((block == 0) & is_last)
        def _():
            for i in range(last):
                scatter_end(seq, i).wait_send()

        @pl.when(block > 0)
        def _():
            for i in range(1, COARSEN):
                give_share(seq, i).wait_send()
            give_back(seq).wait_send()

        @pl.when(has_next)
        def _():
            for i in range(COARSEN):
                give_ahead(seq, i).wait_send()

        @pl.when(jnp.logical_not(has_next))
        def _():
            for i in range(1, COARSEN):
                give_own(seq, i).wait_send()


def hand_over(states, coarse, states_out, coarse_out, sem):
    copies = [
        pltpu.make_async_copy(source, target, sem.at[i])
        for i, (source, target) in enumerate(
            (source.at[0, part], target.at[0, part])
            for source, target in ((states, states_out), (coarse, coarse_out))
            for part in range(states.shape[1])
        )
    ]
    for copy in copies:
        copy.start()
    for copy in copies:
        copy.wait()


def solution(mesh):
    blocks = mesh.shape["depth"] // COARSEN

    def on_device(inputs, attn_in, attn_out, mlp_in, mlp_out, norm_gain, head_gain):
        whole = inputs.shape
        micro, frames, width = whole[0] * PIECES, whole[1] // PIECES, whole[2]
        rows = frames // COARSEN
        state = (micro, frames, width)
        out = jax.ShapeDtypeStruct((1,) + state, jnp.float32)
        vmem = pl.BlockSpec(memory_space=pltpu.VMEM)
        dma = pltpu.SemaphoreType.DMA
        weights = (attn_in, attn_out, mlp_in, mlp_out, norm_gain, head_gain)
        results = pl.pallas_call(
            functools.partial(kernel, blocks),
            out_shape=(out, out),
            in_specs=[pl.BlockSpec(memory_space=pl.ANY)] * 7,
            out_specs=(vmem, vmem),
            scratch_shapes=[
                *(pltpu.VMEM(weight.shape, weight.dtype) for weight in weights),
                pltpu.VMEM(whole[1:], jnp.bfloat16),
                pltpu.VMEM(whole[1:], jnp.bfloat16),
                dma((len(weights) + 3,)),
                pltpu.VMEM((STAGES,) + state, jnp.float32),
                pltpu.VMEM((STAGES,) + state, jnp.float32),
                pltpu.VMEM(state, jnp.float32),
                pltpu.VMEM(state, jnp.float32),
                pltpu.VMEM(state, jnp.float32),
                pltpu.VMEM((micro, rows, width), jnp.float32),
                pltpu.VMEM((micro, COARSEN - 1, rows, width), jnp.float32),
                pltpu.VMEM(state, jnp.float32),
                pltpu.VMEM((GROUP, GROUP), jnp.bfloat16),
                pltpu.VMEM((1, width), jnp.float32),
                pltpu.VMEM((1, width), jnp.float32),
                dma((STAGES, micro)),
                dma((STAGES, micro)),
                dma((micro, COARSEN - 1)),
                dma((micro,)),
                dma((micro, COARSEN)),
                dma((micro, COARSEN - 1)),
                dma((micro,)),
                dma((micro,)),
            ],
            compiler_params=pltpu.CompilerParams(
                collective_id=0, has_side_effects=True, vmem_limit_bytes=56_000_000,
            ),
        )(*(pltpu.with_memory_space_constraint(v, pltpu.HBM) for v in (inputs.reshape(state), *weights)))
        return pl.pallas_call(
            hand_over,
            out_shape=(jax.ShapeDtypeStruct((1,) + whole, jnp.float32),) * 2,
            in_specs=[pl.BlockSpec(memory_space=pl.ANY)] * 2,
            out_specs=(pl.BlockSpec(memory_space=pltpu.HBM),) * 2,
            scratch_shapes=[dma((2 * whole[0],))],
            compiler_params=pltpu.CompilerParams(vmem_limit_bytes=1_000_000),
        )(*(result.reshape((1,) + whole) for result in results))

    in_specs = (
        P("batch", None, None),
        P("depth", None, None),
        P("depth", None, None),
        P("depth", None, None),
        P("depth", None, None),
        P("depth", None),
        P("depth", None),
    )
    out_specs = (P("depth", "batch", None, None), P("depth", "batch", None, None))
    return jax.shard_map(
        on_device, mesh=mesh, in_specs=in_specs, out_specs=out_specs, check_vma=False
    )
```

```python
import functools
import math

import jax
import jax.numpy as jnp
from jax import lax
from jax.experimental import pallas as pl
from jax.experimental.pallas import tpu as pltpu
from jax.sharding import PartitionSpec as P

COARSEN = 4
GROUP = 256
PIECES = 2
LAG = 4

step_size = 0.25
epsilon = 1e-06

FIRST, CHAIN, COARSE, RELAX, FINAL = range(5)
STAGES = 5
MESH = pl.DeviceIdType.MESH


def kernel(
    blocks, inputs, h_qkv, h_out, h_up, h_down, h_gain, h_head, states, coarse,
    w_qkv, w_out, w_up, w_down, in_gain, qk_gain, keys_ref, values_ref, load_sem, rx, tx, base, ends, term, share, parts, same_head, head_scale, query_scale,
    send_sem, recv_sem, share_send, share_recv, ahead_send, own_send, own_recv, back_send,
):
    micro, frames, width = inputs.shape
    gathered = coarse.at[0]
    head_dim = qk_gain.shape[1]
    rows = frames // COARSEN
    device = lax.axis_index("depth")
    position = lax.rem(device, COARSEN)
    block = device // COARSEN
    has_next = block < blocks - 1
    last = COARSEN - 1
    is_last = position == last

    def columns(ref, part):
        return ref.at[0, :, pl.ds(part * width, width)]

    loads = [
        pltpu.make_async_copy(source, target, load_sem.at[i])
        for i, (source, target) in enumerate((
            (h_head, qk_gain), (h_gain, in_gain), (inputs, rx.at[FIRST]),
            *((columns(h_qkv, part), columns(w_qkv, part)) for part in (1, 0, 2)),
            (h_up, w_up), (h_down, w_down), (h_out, w_out),
        ))
    ]
    load_keys, load_queries, load_values, load_up, load_down, load_out = loads[3:]
    for load in loads:
        load.start()

    def at(depth):
        return {"depth": depth}

    barrier = pltpu.get_barrier_semaphore()
    for i in range(COARSEN):
        @pl.when(block > 0)
        def _():
            pl.semaphore_signal(barrier, inc=1, device_id=at((block - 1) * COARSEN + i), device_id_type=MESH)

        @pl.when(has_next)
        def _():
            pl.semaphore_signal(barrier, inc=1, device_id=at((block + 1) * COARSEN + i), device_id_type=MESH)

    for i in range(1, COARSEN):
        other = block * COARSEN + lax.rem(position + i, COARSEN)
        pl.semaphore_signal(barrier, inc=1, device_id=at(other), device_id_type=MESH)

    heads_of = lax.broadcasted_iota(jnp.int32, (GROUP, GROUP), 0) // head_dim
    heads_at = lax.broadcasted_iota(jnp.int32, (GROUP, GROUP), 1) // head_dim
    same_head[...] = jnp.where(heads_of == heads_at, 1.0, 0.0).astype(jnp.bfloat16)
    keys_ref[...] = jnp.zeros_like(keys_ref)
    values_ref[...] = jnp.zeros_like(values_ref)
    loads[0].wait()
    head_scale[...] = jnp.concatenate([qk_gain[...]] * (width // head_dim), axis=1)
    query_scale[...] = head_scale[...] * (math.log2(math.e) / math.sqrt(head_dim))

    neighbours = (block > 0).astype(jnp.int32) + has_next.astype(jnp.int32)
    loads[1].wait()
    loads[2].wait()

    def keep(value, load):
        return value

    def fetched(value, load):
        load.wait()
        return value

    def delta(current, unit, after=keep):
        piece = lax.rem(unit, PIECES)
        here = pl.ds(pl.multiple_of(piece * frames, frames), frames)
        spread = jnp.mean(current * current, axis=-1, keepdims=True) + epsilon
        row_scale = lax.rsqrt(spread)
        gained = (current * in_gain[...]).astype(jnp.bfloat16)
        same = same_head[...]
        copies = GROUP // head_dim
        causal = lax.broadcasted_iota(jnp.int32, (frames, GROUP), 0) + piece * frames >= lax.rem(
            lax.broadcasted_iota(jnp.int32, (frames, GROUP), 1), PIECES * frames
        )
        starts = range(0, width, GROUP)
        half = w_up.shape[2] // 2

        def project(part, load):
            return jnp.dot(
                after(gained, load), w_qkv[0, :, part * width:(part + 1) * width], preferred_element_type=jnp.float32
            )

        def head_norm(rows_of, scale_of):
            cut = [rows_of[:, start:start + GROUP] for start in starts]
            squares = jnp.concatenate([(part * part).astype(jnp.bfloat16) for part in cut], axis=0)
            means = jnp.dot(squares, same, preferred_element_type=jnp.float32) * (1.0 / head_dim)
            scales = lax.rsqrt(means + jnp.concatenate([epsilon * spread] * len(cut), axis=0))
            return [
                (part * (scales[i * frames:(i + 1) * frames] * scale_of[:, start:start + GROUP])).astype(jnp.bfloat16)
                for i, (part, start) in enumerate(zip(cut, starts))
            ]

        def raise_half(i):
            raised = jnp.dot(gained, w_up[0, :, i * half:(i + 1) * half], preferred_element_type=jnp.float32)
            return jax.nn.gelu(raised * row_scale, approximate=True).astype(jnp.bfloat16)

        key_rows = project(1, load_keys)
        query_rows = project(0, load_queries)
        keys_of = head_norm(key_rows, head_scale)
        queries_of = head_norm(query_rows, query_scale)
        values_of = (project(2, load_values) * row_scale).astype(jnp.bfloat16)
        after(gained, load_up)
        hidden = raise_half(0)
        weights, mixes = [], []
        for i, start in enumerate(starts):
            part = slice(start, start + GROUP)
            keys_ref[here, part] = keys_of[i]
            values_ref[here, part] = values_of[:, part]
            keys = jnp.concatenate([keys_ref[:, part]] * copies, axis=0) * same
            scores = lax.dot_general(
                queries_of[i], keys, (((1,), (1,)), ((), ())), preferred_element_type=jnp.float32
            )
            weights.append(jnp.exp2(jnp.where(causal, scores, -jnp.inf)).astype(jnp.bfloat16))
        hidden = jnp.concatenate([hidden, raise_half(1)], axis=1)
        totals = jnp.dot(jnp.concatenate(weights, axis=0), same, preferred_element_type=jnp.float32)
        for weight, start in zip(weights, starts):
            values = jnp.concatenate([values_ref[:, start:start + GROUP]] * copies, axis=0) * same
            mixes.append(jnp.dot(weight, values, preferred_element_type=jnp.float32))
        after(hidden, load_down)
        lowered = jnp.dot(hidden, w_down[0], preferred_element_type=jnp.float32)
        contexts = [
            (mixed / totals[i * frames:(i + 1) * frames]).astype(jnp.bfloat16)
            for i, mixed in enumerate(mixes)
        ]
        context = jnp.concatenate(contexts, axis=1)
        after(context, load_out)
        return jnp.dot(context, w_out[0], preferred_element_type=jnp.float32) + lowered

    def active(stage):
        return (
            ((stage == FIRST) & ((block > 0) | (position == 0)))
            | ((stage == CHAIN) & (position > 0))
            | ((stage == COARSE) & (block > 0))
            | ((stage == RELAX) & (block > 0) & (position > 0))
            | ((stage == FINAL) & (block > 1) & (position < last))
        )

    def passes_on(stage):
        return (
            ((stage == FIRST) & (position == 0))
            | ((stage == CHAIN) & (position > 0) & (position < last))
            | ((stage == COARSE) & (block > 0) & (position == 0))
            | ((stage == RELAX) & (block > 0) & (position > 0) & ((position < last) | has_next))
            | ((stage == FINAL) & (block > 1) & (position < last - 1))
        )

    def is_state(stage):
        return (
            ((stage <= CHAIN) & (block == 0))
            | (((stage == COARSE) | (stage == RELAX)) & (block == 1))
            | ((stage == RELAX) & is_last)
            | (stage == FINAL)
        )

    def hop(stage, seq):
        target = jnp.where(
            stage <= CHAIN, CHAIN, jnp.where((stage == FINAL) | ((stage == RELAX) & is_last), FINAL, RELAX)
        )
        return pltpu.make_async_remote_copy(
            src_ref=tx.at[stage, seq], dst_ref=rx.at[target, seq],
            send_sem=send_sem.at[stage, seq], recv_sem=recv_sem.at[target, seq],
            device_id=at(device + 1), device_id_type=MESH,
        )

    def own_rows(of):
        return pl.ds(pl.multiple_of(of * rows, rows), rows)

    def far_first(i):
        far = last - position
        return (far, lax.rem(position + 2, COARSEN), lax.rem(far + 2, COARSEN), position)[i]

    def give_share(seq, i):
        other = far_first(i - 1)
        return pltpu.make_async_remote_copy(
            src_ref=term.at[seq, own_rows(other)], dst_ref=parts.at[seq, i - 1],
            send_sem=share_send.at[seq, i - 1], recv_sem=share_recv.at[seq],
            device_id=at(block * COARSEN + other), device_id_type=MESH,
        )

    def scatter_end(seq, i):
        return pltpu.make_async_remote_copy(
            src_ref=term.at[seq, own_rows(i)], dst_ref=parts.at[seq, 0],
            send_sem=share_send.at[seq, i], recv_sem=share_recv.at[seq],
            device_id=at(i), device_id_type=MESH,
        )

    def give_ahead(seq, i):
        other = far_first(i)
        return pltpu.make_async_remote_copy(
            src_ref=share.at[seq], dst_ref=rx.at[COARSE, seq, own_rows(position)],
            send_sem=ahead_send.at[seq, i], recv_sem=recv_sem.at[COARSE, seq],
            device_id=at((block + 1) * COARSEN + other), device_id_type=MESH,
        )

    def give_own(seq, i):
        other = far_first(i - 1)
        return pltpu.make_async_remote_copy(
            src_ref=share.at[seq], dst_ref=gathered.at[seq, own_rows(position)],
            send_sem=own_send.at[seq, i - 1], recv_sem=own_recv.at[seq],
            device_id=at(block * COARSEN + other), device_id_type=MESH,
        )

    def landed(ref, sem):
        pltpu.make_async_copy(ref, ref, sem).wait()

    def give_back(seq):
        return pltpu.make_async_remote_copy(
            src_ref=rx.at[COARSE, seq], dst_ref=gathered.at[seq],
            send_sem=back_send.at[seq], recv_sem=own_recv.at[seq],
            device_id=at(device - COARSEN), device_id_type=MESH,
        )

    def finish(seq):
        mine = own_rows(position)

        @pl.when((block == 0) & is_last)
        def _():
            share[seq] = term[seq, mine]

        @pl.when((block == 0) & jnp.logical_not(is_last))
        def _():
            landed(parts.at[seq, 0], share_recv.at[seq])
            share[seq] = parts[seq, 0]

        @pl.when(block > 0)
        def _():
            landed(parts.at[seq], share_recv.at[seq])
            share[seq] = (term[seq, mine] + parts[seq, 0]) + (parts[seq, 1] + parts[seq, 2])

        @pl.when(has_next)
        def _():
            for i in range(COARSEN):
                give_ahead(seq, i).start()

        @pl.when(jnp.logical_not(has_next))
        def _():
            for i in range(1, COARSEN):
                give_own(seq, i).start()
            gathered[seq, mine] = share[seq]

    def turn(step, carry):
        stage, seq = step // micro, lax.rem(step, micro)

        @pl.when(active(stage))
        def _():
            @pl.when(stage > FIRST)
            def _():
                landed(rx.at[stage, seq], recv_sem.at[stage, seq])

            current = rx[stage, seq]
            change = step_size * delta(current, seq)
            moved = current + change

            shares_first = (stage == COARSE) & (block == 1)

            @pl.when(passes_on(stage) & jnp.logical_not(shares_first))
            def _():
                tx[stage, seq] = moved
                hop(stage, seq).start()

            @pl.when(stage == FIRST)
            def _():
                base[seq] = change

            @pl.when((stage == CHAIN) & is_last)
            def _():
                @pl.when(block == 0)
                def _():
                    term[seq] = moved
                    for i in range(last):
                        scatter_end(seq, i).start()
                    finish(seq)

                @pl.when(block > 0)
                def _():
                    ends[seq] = moved - rx[FIRST, seq]

            @pl.when(stage == COARSE)
            def _():
                increment = change - base[seq]

                @pl.when(is_last)
                def _():
                    term[seq] = increment + (ends[seq] + current)

                @pl.when(jnp.logical_not(is_last))
                def _():
                    term[seq] = increment

                for i in range(1, COARSEN):
                    give_share(seq, i).start()

                @pl.when(passes_on(stage) & shares_first)
                def _():
                    tx[stage, seq] = moved
                    hop(stage, seq).start()

                give_back(seq).start()

            @pl.when(is_state(stage))
            def _():
                states[0, seq] = moved

            since = step - COARSE * micro - LAG
            turns = jnp.where((position == 1) & (block > 1), micro, micro - LAG)

            @pl.when((block > 0) & (since >= 0) & (since < turns))
            def _():
                finish(since)

        return carry

    def finish_left(first, last_seq, when):
        for seq in range(first, last_seq):
            @pl.when(when)
            def _():
                finish(seq)

    current = rx[FIRST, 0]
    change = step_size * delta(current, 0, fetched)
    base[0] = change
    pl.semaphore_wait(barrier, COARSEN - 1 + COARSEN * neighbours)
    moved = current + change

    @pl.when(position == 0)
    def _():
        tx[FIRST, 0] = moved
        hop(FIRST, 0).start()

    @pl.when(block == 0)
    def _():
        states[0, 0] = moved

    lax.fori_loop(1, RELAX * micro, turn, 0)
    finish_left(0, micro, (block == 0) & jnp.logical_not(is_last))
    finish_left(max(micro - LAG, 0), micro, (block == 1) | ((block > 1) & (position != 1)))
    lax.fori_loop(RELAX * micro, STAGES * micro, turn, 0)

    for seq in range(micro):
        @pl.when(has_next)
        def _():
            landed(gathered.at[seq], own_recv.at[seq])

        @pl.when(jnp.logical_not(has_next))
        def _():
            landed(gathered.at[seq, pl.ds(0, last * rows)], own_recv.at[seq])

    for seq in range(micro):
        for stage in range(STAGES):
            @pl.when(passes_on(stage))
            def _():
                hop(stage, seq).wait_send()

        @pl.when((block == 0) & is_last)
        def _():
            for i in range(last):
                scatter_end(seq, i).wait_send()

        @pl.when(block > 0)
        def _():
            for i in range(1, COARSEN):
                give_share(seq, i).wait_send()
            give_back(seq).wait_send()

        @pl.when(has_next)
        def _():
            for i in range(COARSEN):
                give_ahead(seq, i).wait_send()

        @pl.when(jnp.logical_not(has_next))
        def _():
            for i in range(1, COARSEN):
                give_own(seq, i).wait_send()


def hand_over(states, coarse, states_out, coarse_out, sem):
    copies = [
        pltpu.make_async_copy(source, target, sem.at[i])
        for i, (source, target) in enumerate(
            (source.at[0, part], target.at[0, part])
            for source, target in ((states, states_out), (coarse, coarse_out))
            for part in range(states.shape[1])
        )
    ]
    for copy in copies:
        copy.start()
    for copy in copies:
        copy.wait()


def solution(mesh):
    blocks = mesh.shape["depth"] // COARSEN

    def on_device(inputs, attn_in, attn_out, mlp_in, mlp_out, norm_gain, head_gain):
        whole = inputs.shape
        micro, frames, width = whole[0] * PIECES, whole[1] // PIECES, whole[2]
        rows = frames // COARSEN
        state = (micro, frames, width)
        out = jax.ShapeDtypeStruct((1,) + state, jnp.float32)
        vmem = pl.BlockSpec(memory_space=pltpu.VMEM)
        dma = pltpu.SemaphoreType.DMA
        weights = (attn_in, attn_out, mlp_in, mlp_out, norm_gain, head_gain)
        results = pl.pallas_call(
            functools.partial(kernel, blocks),
            out_shape=(out, out),
            in_specs=[pl.BlockSpec(memory_space=pl.ANY)] * 7,
            out_specs=(vmem, vmem),
            scratch_shapes=[
                *(pltpu.VMEM(weight.shape, weight.dtype) for weight in weights),
                pltpu.VMEM(whole[1:], jnp.bfloat16),
                pltpu.VMEM(whole[1:], jnp.bfloat16),
                dma((len(weights) + 3,)),
                pltpu.VMEM((STAGES,) + state, jnp.float32),
                pltpu.VMEM((STAGES,) + state, jnp.float32),
                pltpu.VMEM(state, jnp.float32),
                pltpu.VMEM(state, jnp.float32),
                pltpu.VMEM(state, jnp.float32),
                pltpu.VMEM((micro, rows, width), jnp.float32),
                pltpu.VMEM((micro, COARSEN - 1, rows, width), jnp.float32),
                pltpu.VMEM((GROUP, GROUP), jnp.bfloat16),
                pltpu.VMEM((1, width), jnp.float32),
                pltpu.VMEM((1, width), jnp.float32),
                dma((STAGES, micro)),
                dma((STAGES, micro)),
                dma((micro, COARSEN - 1)),
                dma((micro,)),
                dma((micro, COARSEN)),
                dma((micro, COARSEN - 1)),
                dma((micro,)),
                dma((micro,)),
            ],
            compiler_params=pltpu.CompilerParams(
                collective_id=0, has_side_effects=True, vmem_limit_bytes=56_000_000,
            ),
        )(*(pltpu.with_memory_space_constraint(v, pltpu.HBM) for v in (inputs.reshape(state), *weights)))
        return pl.pallas_call(
            hand_over,
            out_shape=(jax.ShapeDtypeStruct((1,) + whole, jnp.float32),) * 2,
            in_specs=[pl.BlockSpec(memory_space=pl.ANY)] * 2,
            out_specs=(pl.BlockSpec(memory_space=pltpu.HBM),) * 2,
            scratch_shapes=[dma((2 * whole[0],))],
            compiler_params=pltpu.CompilerParams(vmem_limit_bytes=1_000_000),
        )(*(result.reshape((1,) + whole) for result in results))

    in_specs = (
        P("batch", None, None),
        P("depth", None, None),
        P("depth", None, None),
        P("depth", None, None),
        P("depth", None, None),
        P("depth", None),
        P("depth", None),
    )
    out_specs = (P("depth", "batch", None, None), P("depth", "batch", None, None))
    return jax.shard_map(
        on_device, mesh=mesh, in_specs=in_specs, out_specs=out_specs, check_vma=False
    )
```

```python
import functools
import math

import jax
import jax.numpy as jnp
from jax import lax
from jax.experimental import pallas as pl
from jax.experimental.pallas import tpu as pltpu
from jax.sharding import PartitionSpec as P

COARSEN = 4
GROUP = 256
PIECES = 2
LAG = 4

step_size = 0.25
epsilon = 1e-06

FIRST, CHAIN, COARSE, RELAX, FINAL = range(5)
STAGES = 5
MESH = pl.DeviceIdType.MESH


def kernel(
    blocks, inputs, h_qkv, h_out, h_up, h_down, h_gain, h_head, states, coarse,
    w_qkv, w_out, w_up, w_down, in_gain, qk_gain, keys_ref, values_ref, load_sem, rx, tx, base, ends, term, share, parts, same_head, head_scale, query_scale,
    send_sem, recv_sem, share_send, share_recv, ahead_send, own_send, own_recv, back_send,
):
    micro, frames, width = inputs.shape
    gathered = coarse.at[0]
    head_dim = qk_gain.shape[1]
    rows = frames // COARSEN
    device = lax.axis_index("depth")
    position = lax.rem(device, COARSEN)
    block = device // COARSEN
    has_next = block < blocks - 1
    last = COARSEN - 1
    is_last = position == last

    def columns(ref, part):
        return ref.at[0, :, pl.ds(part * width, width)]

    loads = [
        pltpu.make_async_copy(source, target, load_sem.at[i])
        for i, (source, target) in enumerate((
            (h_head, qk_gain), (h_gain, in_gain), (inputs, rx.at[FIRST]),
            *((columns(h_qkv, part), columns(w_qkv, part)) for part in (1, 0, 2)),
            (h_up, w_up), (h_down, w_down), (h_out, w_out),
        ))
    ]
    load_keys, load_queries, load_values, load_up, load_down, load_out = loads[3:]
    for load in loads:
        load.start()

    def at(depth):
        return {"depth": depth}

    barrier = pltpu.get_barrier_semaphore()
    for i in range(COARSEN):
        @pl.when(block > 0)
        def _():
            pl.semaphore_signal(barrier, inc=1, device_id=at((block - 1) * COARSEN + i), device_id_type=MESH)

        @pl.when(has_next)
        def _():
            pl.semaphore_signal(barrier, inc=1, device_id=at((block + 1) * COARSEN + i), device_id_type=MESH)

    for i in range(1, COARSEN):
        other = block * COARSEN + lax.rem(position + i, COARSEN)
        pl.semaphore_signal(barrier, inc=1, device_id=at(other), device_id_type=MESH)

    heads_of = lax.broadcasted_iota(jnp.int32, (GROUP, GROUP), 0) // head_dim
    heads_at = lax.broadcasted_iota(jnp.int32, (GROUP, GROUP), 1) // head_dim
    same_head[...] = jnp.where(heads_of == heads_at, 1.0, 0.0).astype(jnp.bfloat16)
    keys_ref[...] = jnp.zeros_like(keys_ref)
    values_ref[...] = jnp.zeros_like(values_ref)
    loads[0].wait()
    head_scale[...] = jnp.concatenate([qk_gain[...]] * (width // head_dim), axis=1)
    query_scale[...] = head_scale[...] * (math.log2(math.e) / math.sqrt(head_dim))

    neighbours = (block > 0).astype(jnp.int32) + has_next.astype(jnp.int32)
    loads[1].wait()
    loads[2].wait()

    def keep(value, load):
        return value

    def fetched(value, load):
        load.wait()
        return value

    def delta(current, unit, after=keep):
        piece = lax.rem(unit, PIECES)
        here = pl.ds(pl.multiple_of(piece * frames, frames), frames)
        spread = jnp.mean(current * current, axis=-1, keepdims=True) + epsilon
        row_scale = lax.rsqrt(spread)
        gained = (current * in_gain[...]).astype(jnp.bfloat16)
        same = same_head[...]
        copies = GROUP // head_dim
        causal = lax.broadcasted_iota(jnp.int32, (frames, GROUP), 0) + piece * frames >= lax.rem(
            lax.broadcasted_iota(jnp.int32, (frames, GROUP), 1), PIECES * frames
        )
        starts = range(0, width, GROUP)
        half = w_up.shape[2] // 2

        def project(part, load):
            return jnp.dot(
                after(gained, load), w_qkv[0, :, part * width:(part + 1) * width], preferred_element_type=jnp.float32
            )

        def head_norm(rows_of, scale_of):
            cut = [rows_of[:, start:start + GROUP] for start in starts]
            squares = jnp.concatenate([(part * part).astype(jnp.bfloat16) for part in cut], axis=0)
            means = jnp.dot(squares, same, preferred_element_type=jnp.float32) * (1.0 / head_dim)
            scales = lax.rsqrt(means + jnp.concatenate([epsilon * spread] * len(cut), axis=0))
            return [
                (part * (scales[i * frames:(i + 1) * frames] * scale_of[:, start:start + GROUP])).astype(jnp.bfloat16)
                for i, (part, start) in enumerate(zip(cut, starts))
            ]

        def raise_half(i):
            raised = jnp.dot(gained, w_up[0, :, i * half:(i + 1) * half], preferred_element_type=jnp.float32)
            return jax.nn.gelu(raised * row_scale, approximate=True).astype(jnp.bfloat16)

        key_rows = project(1, load_keys)
        query_rows = project(0, load_queries)
        keys_of = head_norm(key_rows, head_scale)
        queries_of = head_norm(query_rows, query_scale)
        values_of = (project(2, load_values) * row_scale).astype(jnp.bfloat16)
        after(gained, load_up)
        hidden = raise_half(0)
        weights, mixes = [], []
        for i, start in enumerate(starts):
            part = slice(start, start + GROUP)
            keys_ref[here, part] = keys_of[i]
            values_ref[here, part] = values_of[:, part]
            keys = jnp.concatenate([keys_ref[:, part]] * copies, axis=0) * same
            scores = lax.dot_general(
                queries_of[i], keys, (((1,), (1,)), ((), ())), preferred_element_type=jnp.float32
            )
            weights.append(jnp.exp2(jnp.where(causal, scores, -jnp.inf)).astype(jnp.bfloat16))
        hidden = jnp.concatenate([hidden, raise_half(1)], axis=1)
        totals = jnp.dot(jnp.concatenate(weights, axis=0), same, preferred_element_type=jnp.float32)
        for weight, start in zip(weights, starts):
            values = jnp.concatenate([values_ref[:, start:start + GROUP]] * copies, axis=0) * same
            mixes.append(jnp.dot(weight, values, preferred_element_type=jnp.float32))
        after(hidden, load_down)
        lowered = jnp.dot(hidden, w_down[0], preferred_element_type=jnp.float32)
        contexts = [
            (mixed / totals[i * frames:(i + 1) * frames]).astype(jnp.bfloat16)
            for i, mixed in enumerate(mixes)
        ]
        context = jnp.concatenate(contexts, axis=1)
        after(context, load_out)
        return jnp.dot(context, w_out[0], preferred_element_type=jnp.float32) + lowered

    def active(stage):
        return (
            ((stage == FIRST) & ((block > 0) | (position == 0)))
            | ((stage == CHAIN) & (position > 0))
            | ((stage == COARSE) & (block > 0))
            | ((stage == RELAX) & (block > 0) & (position > 0))
            | ((stage == FINAL) & (block > 1) & (position < last))
        )

    def passes_on(stage):
        return (
            ((stage == FIRST) & (position == 0))
            | ((stage == CHAIN) & (position > 0) & (position < last))
            | ((stage == COARSE) & (block > 0) & (position == 0))
            | ((stage == RELAX) & (block > 0) & (position > 0) & ((position < last) | has_next))
            | ((stage == FINAL) & (block > 1) & (position < last - 1))
        )

    def is_state(stage):
        return (
            ((stage <= CHAIN) & (block == 0))
            | (((stage == COARSE) | (stage == RELAX)) & (block == 1))
            | ((stage == RELAX) & is_last)
            | (stage == FINAL)
        )

    def hop(stage, seq):
        target = jnp.where(
            stage <= CHAIN, CHAIN, jnp.where((stage == FINAL) | ((stage == RELAX) & is_last), FINAL, RELAX)
        )
        return pltpu.make_async_remote_copy(
            src_ref=tx.at[stage, seq], dst_ref=rx.at[target, seq],
            send_sem=send_sem.at[stage, seq], recv_sem=recv_sem.at[target, seq],
            device_id=at(device + 1), device_id_type=MESH,
        )

    def own_rows(of):
        return pl.ds(pl.multiple_of(of * rows, rows), rows)

    def far_first(i):
        far = last - position
        return (far, lax.rem(position + 2, COARSEN), lax.rem(far + 2, COARSEN), position)[i]

    def give_share(seq, i):
        other = far_first(i - 1)
        return pltpu.make_async_remote_copy(
            src_ref=term.at[seq, own_rows(other)], dst_ref=parts.at[seq, i - 1],
            send_sem=share_send.at[seq, i - 1], recv_sem=share_recv.at[seq],
            device_id=at(block * COARSEN + other), device_id_type=MESH,
        )

    def scatter_end(seq, i):
        return pltpu.make_async_remote_copy(
            src_ref=term.at[seq, own_rows(i)], dst_ref=parts.at[seq, 0],
            send_sem=share_send.at[seq, i], recv_sem=share_recv.at[seq],
            device_id=at(i), device_id_type=MESH,
        )

    def give_ahead(seq, i):
        other = far_first(i)
        return pltpu.make_async_remote_copy(
            src_ref=share.at[seq], dst_ref=rx.at[COARSE, seq, own_rows(position)],
            send_sem=ahead_send.at[seq, i], recv_sem=recv_sem.at[COARSE, seq],
            device_id=at((block + 1) * COARSEN + other), device_id_type=MESH,
        )

    def give_own(seq, i):
        other = far_first(i - 1)
        return pltpu.make_async_remote_copy(
            src_ref=share.at[seq], dst_ref=gathered.at[seq, own_rows(position)],
            send_sem=own_send.at[seq, i - 1], recv_sem=own_recv.at[seq],
            device_id=at(block * COARSEN + other), device_id_type=MESH,
        )

    def landed(ref, sem):
        pltpu.make_async_copy(ref, ref, sem).wait()

    def give_back(seq):
        return pltpu.make_async_remote_copy(
            src_ref=rx.at[COARSE, seq], dst_ref=gathered.at[seq],
            send_sem=back_send.at[seq], recv_sem=own_recv.at[seq],
            device_id=at(device - COARSEN), device_id_type=MESH,
        )

    def finish(seq):
        mine = own_rows(position)

        @pl.when((block == 0) & is_last)
        def _():
            share[seq] = term[seq, mine]

        @pl.when((block == 0) & jnp.logical_not(is_last))
        def _():
            landed(parts.at[seq, 0], share_recv.at[seq])
            share[seq] = parts[seq, 0]

        @pl.when(block > 0)
        def _():
            landed(parts.at[seq], share_recv.at[seq])
            share[seq] = (term[seq, mine] + parts[seq, 0]) + (parts[seq, 1] + parts[seq, 2])

        @pl.when(has_next)
        def _():
            for i in range(COARSEN):
                give_ahead(seq, i).start()

        @pl.when(jnp.logical_not(has_next))
        def _():
            for i in range(1, COARSEN):
                give_own(seq, i).start()
            gathered[seq, mine] = share[seq]

    def turn(step, carry):
        stage, seq = step // micro, lax.rem(step, micro)

        @pl.when(active(stage))
        def _():
            @pl.when(stage > FIRST)
            def _():
                landed(rx.at[stage, seq], recv_sem.at[stage, seq])

            current = rx[stage, seq]
            change = step_size * delta(current, seq)
            moved = current + change

            shares_first = stage == COARSE

            @pl.when(passes_on(stage) & jnp.logical_not(shares_first))
            def _():
                tx[stage, seq] = moved
                hop(stage, seq).start()

            @pl.when(stage == FIRST)
            def _():
                base[seq] = change

            @pl.when((stage == CHAIN) & is_last)
            def _():
                @pl.when(block == 0)
                def _():
                    term[seq] = moved
                    for i in range(last):
                        scatter_end(seq, i).start()
                    finish(seq)

                @pl.when(block > 0)
                def _():
                    ends[seq] = moved - rx[FIRST, seq]

            @pl.when(stage == COARSE)
            def _():
                increment = change - base[seq]

                @pl.when(is_last)
                def _():
                    term[seq] = increment + (ends[seq] + current)

                @pl.when(jnp.logical_not(is_last))
                def _():
                    term[seq] = increment

                for i in range(1, COARSEN):
                    give_share(seq, i).start()

                @pl.when(passes_on(stage) & shares_first)
                def _():
                    tx[stage, seq] = moved
                    hop(stage, seq).start()

                give_back(seq).start()

            @pl.when(is_state(stage))
            def _():
                states[0, seq] = moved

            since = step - COARSE * micro - LAG
            turns = jnp.where((position == 1) & (block > 1), micro, micro - LAG)

            @pl.when((block > 0) & (since >= 0) & (since < turns))
            def _():
                finish(since)

        return carry

    def finish_left(first, last_seq, when):
        for seq in range(first, last_seq):
            @pl.when(when)
            def _():
                finish(seq)

    current = rx[FIRST, 0]
    change = step_size * delta(current, 0, fetched)
    base[0] = change
    pl.semaphore_wait(barrier, COARSEN - 1 + COARSEN * neighbours)
    moved = current + change

    @pl.when(position == 0)
    def _():
        tx[FIRST, 0] = moved
        hop(FIRST, 0).start()

    @pl.when(block == 0)
    def _():
        states[0, 0] = moved

    lax.fori_loop(1, RELAX * micro, turn, 0)
    finish_left(0, micro, (block == 0) & jnp.logical_not(is_last))
    finish_left(max(micro - LAG, 0), micro, (block == 1) | ((block > 1) & (position != 1)))
    lax.fori_loop(RELAX * micro, STAGES * micro, turn, 0)

    for seq in range(micro):
        @pl.when(has_next)
        def _():
            landed(gathered.at[seq], own_recv.at[seq])

        @pl.when(jnp.logical_not(has_next))
        def _():
            landed(gathered.at[seq, pl.ds(0, last * rows)], own_recv.at[seq])

    for seq in range(micro):
        for stage in range(STAGES):
            @pl.when(passes_on(stage))
            def _():
                hop(stage, seq).wait_send()

        @pl.when((block == 0) & is_last)
        def _():
            for i in range(last):
                scatter_end(seq, i).wait_send()

        @pl.when(block > 0)
        def _():
            for i in range(1, COARSEN):
                give_share(seq, i).wait_send()
            give_back(seq).wait_send()

        @pl.when(has_next)
        def _():
            for i in range(COARSEN):
                give_ahead(seq, i).wait_send()

        @pl.when(jnp.logical_not(has_next))
        def _():
            for i in range(1, COARSEN):
                give_own(seq, i).wait_send()


def hand_over(states, coarse, states_out, coarse_out, sem):
    copies = [
        pltpu.make_async_copy(source, target, sem.at[i])
        for i, (source, target) in enumerate(
            (source.at[0, part], target.at[0, part])
            for source, target in ((states, states_out), (coarse, coarse_out))
            for part in range(states.shape[1])
        )
    ]
    for copy in copies:
        copy.start()
    for copy in copies:
        copy.wait()


def solution(mesh):
    blocks = mesh.shape["depth"] // COARSEN

    def on_device(inputs, attn_in, attn_out, mlp_in, mlp_out, norm_gain, head_gain):
        whole = inputs.shape
        micro, frames, width = whole[0] * PIECES, whole[1] // PIECES, whole[2]
        rows = frames // COARSEN
        state = (micro, frames, width)
        out = jax.ShapeDtypeStruct((1,) + state, jnp.float32)
        vmem = pl.BlockSpec(memory_space=pltpu.VMEM)
        dma = pltpu.SemaphoreType.DMA
        weights = (attn_in, attn_out, mlp_in, mlp_out, norm_gain, head_gain)
        results = pl.pallas_call(
            functools.partial(kernel, blocks),
            out_shape=(out, out),
            in_specs=[pl.BlockSpec(memory_space=pl.ANY)] * 7,
            out_specs=(vmem, vmem),
            scratch_shapes=[
                *(pltpu.VMEM(weight.shape, weight.dtype) for weight in weights),
                pltpu.VMEM(whole[1:], jnp.bfloat16),
                pltpu.VMEM(whole[1:], jnp.bfloat16),
                dma((len(weights) + 3,)),
                pltpu.VMEM((STAGES,) + state, jnp.float32),
                pltpu.VMEM((STAGES,) + state, jnp.float32),
                pltpu.VMEM(state, jnp.float32),
                pltpu.VMEM(state, jnp.float32),
                pltpu.VMEM(state, jnp.float32),
                pltpu.VMEM((micro, rows, width), jnp.float32),
                pltpu.VMEM((micro, COARSEN - 1, rows, width), jnp.float32),
                pltpu.VMEM((GROUP, GROUP), jnp.bfloat16),
                pltpu.VMEM((1, width), jnp.float32),
                pltpu.VMEM((1, width), jnp.float32),
                dma((STAGES, micro)),
                dma((STAGES, micro)),
                dma((micro, COARSEN - 1)),
                dma((micro,)),
                dma((micro, COARSEN)),
                dma((micro, COARSEN - 1)),
                dma((micro,)),
                dma((micro,)),
            ],
            compiler_params=pltpu.CompilerParams(
                collective_id=0, has_side_effects=True, vmem_limit_bytes=56_000_000,
            ),
        )(*(pltpu.with_memory_space_constraint(v, pltpu.HBM) for v in (inputs.reshape(state), *weights)))
        return pl.pallas_call(
            hand_over,
            out_shape=(jax.ShapeDtypeStruct((1,) + whole, jnp.float32),) * 2,
            in_specs=[pl.BlockSpec(memory_space=pl.ANY)] * 2,
            out_specs=(pl.BlockSpec(memory_space=pltpu.HBM),) * 2,
            scratch_shapes=[dma((2 * whole[0],))],
            compiler_params=pltpu.CompilerParams(vmem_limit_bytes=1_000_000),
        )(*(result.reshape((1,) + whole) for result in results))

    in_specs = (
        P("batch", None, None),
        P("depth", None, None),
        P("depth", None, None),
        P("depth", None, None),
        P("depth", None, None),
        P("depth", None),
        P("depth", None),
    )
    out_specs = (P("depth", "batch", None, None), P("depth", "batch", None, None))
    return jax.shard_map(
        on_device, mesh=mesh, in_specs=in_specs, out_specs=out_specs, check_vma=False
    )
```
